32 devices in a mesh: lon: 8 (over z, y), lat: 4 (over x, core).
Axes of the slice: x: 2, y: 2, z: 4, core: 2. Of those that a mesh axis runs over, the one named last changes fastest.
Arguments:
- perturbation: float32 [80, 128, 4096], P(None, 'lon', 'lat'), may hold values from -6 to 6
- weight_table: float32 [8, 2048], P(None, 'lat'), may hold values from 0.1 to 1
- band_index: int32 [13], replicated, may hold values from 0 to 7
Outputs:
- localized: float32 [80, 128, 4096], P(None, 'lon', 'lat')
The draws below stay inside these ranges and needn't reach their ends.
Inputs may be any that keep to these rules, and one draw needn't show every extreme that they name: `band_index`: each entry names a row of weight_table.
All inputs are finite; a program needn't handle non-finite values.
Results may differ from the reference program's by a relative error of at most 0.00005.
Values sent between devices are 32-bit elements; how exact they have to be, the bound alone decides.
No kernel may reach another device: no remote copies, remote signals or barrier semaphores. Data moves between devices by JAX's collectives and lax.ppermute only.
A program may use at most 128 MiB of HBM per device.

```python
import math
import jax
import jax.numpy as jnp
from jax import lax

MEMBERS = 80
LEVELS = 4
TABLE = 8
BANDS = 13
NLON = 128
NLAT = 4096


def touch_ends(drawn, own_key, smallest, largest):
    longest = drawn.shape.index(max(drawn.shape))
    spots = []
    for shift in (0, 1):
        where = [jax.random.randint(jax.random.fold_in(own_key, axis), (), 0, length) for axis, length in enumerate(drawn.shape)]
        where[longest] = (where[longest] + shift) % drawn.shape[longest]
        spots.append(tuple(where))
    return drawn.at[spots[0]].set(smallest).at[spots[1]].set(largest)


def levels(key, shape, pieces, low, largest):
    loudness, own = 1.0, jax.random.fold_in(key, 6)
    for axis_at, shards_of in pieces:
        draws = jnp.exp(jax.random.uniform(jax.random.fold_in(own, axis_at), (shards_of,), jnp.float32, low / len(pieces), largest / len(pieces)))
        loudness = loudness * jnp.repeat(draws, shape[axis_at] // shards_of).reshape([-1 if axis == axis_at else 1 for axis in range(len(shape))])
    return loudness


def noise(rng, shape, deviation, bound, shards=(), dtype=jnp.bfloat16):
    loudness = levels(rng, shape, shards, -0.22, 0.18) if shards else 1.0
    array = jax.random.normal(rng, shape, jnp.float32) * deviation * loudness
    return jnp.minimum(jnp.maximum(array, -bound), bound).astype(dtype)


def setup_inputs(seed: int = 0) -> dict:
    keys = jax.random.split(jax.random.key(seed), 4)
    return {
        "perturbation": noise(keys[0], (MEMBERS, NLON, NLAT), 1.0, 6.0, ((1, 8), (2, 4)), jnp.float32),
        "weight_table": jnp.clip(jnp.exp(math.log(1.0) - 2.3025851 * jax.random.uniform(keys[1], (TABLE, NLAT // 2), jnp.float32) ** levels(keys[1], (TABLE, NLAT // 2), ((1, 4),), -0.2, 0.2)), 0.1, 1.0),
        "band_index": touch_ends(jax.random.randint(keys[2], (BANDS,), 0, TABLE), jax.random.fold_in(keys[2], 1), 0, TABLE - 1).astype(jnp.int32),
    }


root_three = math.sqrt(3.0)
low_taps = [(1.0 + root_three) / (4.0 * math.sqrt(2.0)), (3.0 + root_three) / (4.0 * math.sqrt(2.0)), (3.0 - root_three) / (4.0 * math.sqrt(2.0)), (1.0 - root_three) / (4.0 * math.sqrt(2.0))]
high_taps = [low_taps[3], -low_taps[2], low_taps[1], -low_taps[0]]

def analyze(extended, count, axis, taps):
    result = taps[0] * lax.slice_in_dim(extended, 0, count - 1, 2, axis)
    for tap in range(1, 4):
        result = result + taps[tap] * lax.slice_in_dim(extended, tap, tap + count - 1, 2, axis)
    return result

def synthesize(low, high, prev_low, prev_high, axis):
    even = low_taps[0] * low + low_taps[2] * prev_low + high_taps[0] * high + high_taps[2] * prev_high
    odd = low_taps[1] * low + low_taps[3] * prev_low + high_taps[1] * high + high_taps[3] * prev_high
    paired = jnp.stack([even, odd], axis + 1)
    shape = list(low.shape)
    shape[axis] = shape[axis] * 2
    return paired.reshape(shape)

def profile(weight_table, entry, level):
    return weight_table[entry][::2 ** level][None, None, :]

def lat_split(field):
    extended = jnp.concatenate([field, jnp.zeros(field.shape[:2] + (2,), jnp.float32)], 2)
    count = field.shape[2]
    return (analyze(extended, count, 2, low_taps), analyze(extended, count, 2, high_taps))

def lat_join(low, high):
    zeros = jnp.zeros(low.shape[:2] + (1,), jnp.float32)
    prev_low = jnp.concatenate([zeros, low[:, :, :-1]], 2)
    prev_high = jnp.concatenate([zeros, high[:, :, :-1]], 2)
    return synthesize(low, high, prev_low, prev_high, 2)

def reference(perturbation, weight_table, band_index):
    current = perturbation
    details = []
    for level in range(LEVELS):
        count = current.shape[1]
        extended = jnp.concatenate([current, current[:, :2]], 1)
        lon_low = analyze(extended, count, 1, low_taps)
        lon_high = analyze(extended, count, 1, high_taps)
        coarse, band_zero = lat_split(lon_low)
        band_one, band_two = lat_split(lon_high)
        bands = [band_zero, band_one, band_two]
        details.append([bands[b] * profile(weight_table, band_index[3 * level + b], level) for b in range(3)])
        current = coarse
    current = current * profile(weight_table, band_index[3 * LEVELS], LEVELS - 1)
    for level in reversed(range(LEVELS)):
        bands = details[level]
        lon_low = lat_join(current, bands[0])
        lon_high = lat_join(bands[1], bands[2])
        current = synthesize(lon_low, lon_high, jnp.roll(lon_low, 1, 1), jnp.roll(lon_high, 1, 1), 1)
    return current
```

```python
import math

import jax
import jax.numpy as jnp
from jax import lax
from jax.experimental import pallas as pl
from jax.experimental.pallas import tpu as pltpu
from jax.sharding import PartitionSpec as P

LEVELS = 4
LANES = 128
SUB = 8
HALO = 32

root_three = math.sqrt(3.0)
tap_0 = (1.0 + root_three) / (4.0 * math.sqrt(2.0))
tap_1 = (3.0 + root_three) / (4.0 * math.sqrt(2.0))
tap_2 = (3.0 - root_three) / (4.0 * math.sqrt(2.0))
tap_3 = (1.0 - root_three) / (4.0 * math.sqrt(2.0))
T = tap_3 / tap_2
Q = tap_2 / tap_1


RIGHT = {"h": 0, "g": 4, "c1": 8, "a1": 12, "a2": 16, "k": 18, "edge": 19}
LEFT = {"h": 0, "g": 4, "b1": 8, "b2": 12, "b3": 14, "edge": 15}
RIGHT_SIZE = 20
LEFT_SIZE = 16
TURN = {"h": 0, "c1": 32, "b1": 32, "a1": 64, "a2": 88, "b2": 88, "k": 100, "b3": 100, "g": 106}
COUNT = {"h": 4, "g": 4, "c1": 4, "a1": 4, "b1": 4, "a2": 2, "b2": 2, "k": 1, "b3": 1}
WEIGHTS = {}
WEIGHT_COUNT = 0
for level_at in range(LEVELS):
    for band_at in range(3 if level_at < LEVELS - 1 else 4):
        WEIGHTS[level_at, band_at] = WEIGHT_COUNT
        WEIGHT_COUNT += (5, 3, 2, 1)[level_at]


def lane():
    return lax.broadcasted_iota(jnp.int32, (SUB, LANES), 1)


def turn(v, by):
    by = by % LANES
    return v if by == 0 else pltpu.roll(v, by, 1)


def pick(v, index):
    return jnp.take_along_axis(v, index, axis=1, mode="promise_in_bounds")


class Lanes:
    def __init__(self):
        l = lane()
        self.l = l
        self.even = (l & 1) == 0
        self.sort = jnp.where(l < 64, 2 * l, 2 * l - 127)
        self.unsort = (l >> 1) + 64 * (l & 1)
        self.sort_edge = (2 * l) & 127
        self.unsort_edge = jnp.where(l < 64, l >> 1, 64 + (l >> 1))
        self.ahead = jnp.where(l < 126, l + 2, 127 - l)
        self.behind = jnp.where(l >= 2, l - 2, 127 - l)
        self.behind = jnp.where(l == 0, 127, jnp.where(l == 1, 126, l - 2))
        self.ahead = jnp.where(l == 126, 1, jnp.where(l == 127, 0, l + 2))
        self.first = l == 0
        self.last = l == 127

    def split(self, row):
        main, edge = row[:-1], row[-1]
        evens, odds = [], []
        if len(main) == 1:
            main, alone = row, False
        else:
            alone = True
        for i in range(0, len(main), 2):
            evens.append(jnp.where(self.even, main[i], turn(main[i + 1], 1)))
            odds.append(jnp.where(self.even, turn(main[i], -1), main[i + 1]))
        if alone:
            evens.append(edge)
            odds.append(turn(edge, -1))
        a = [o - T * e for e, o in zip(evens, odds)]
        b = [e + T * o for e, o in zip(evens, odds)]
        if not alone:
            return a, [pick(b[0], self.ahead)]
        shifted = []
        for i in range(len(b) - 1):
            shifted.append(pick(jnp.where(self.first, b[i + 1], b[i]), self.ahead))
        shifted.append(turn(jnp.where(self.first, b[0], b[-1]), -2))
        return a, shifted

    def analyze(self, row):
        a, b = self.split(row)
        return [i + Q * j for i, j in zip(a, b)], [j - Q * i for i, j in zip(a, b)]

    def low(self, row):
        a, b = self.split(row)
        return [i + Q * j for i, j in zip(a, b)]

    def sorted(self, coefs):
        return [pick(v, self.sort) for v in coefs[:-1]] + [pick(coefs[-1], self.sort_edge)]

    def unsorted(self, row):
        if len(row) == 2:
            return [None]
        return [pick(v, self.unsort) for v in row[:-1]] + [pick(row[-1], self.unsort_edge)]

    def join(self, a, b, with_edge=True):
        if len(a) == 1:
            shifted = [pick(b[0], self.behind)]
        else:
            shifted = []
            for i in range(len(b) - 1):
                before = turn(b[-1], 1) if i == 0 else b[i - 1]
                shifted.append(pick(jnp.where(self.last, before, b[i]), self.behind))
            shifted.append(turn(b[-1], 2) if with_edge else None)
        row = []
        pairs = len(a) if len(a) == 1 else len(a) - 1
        for i in range(pairs):
            e = shifted[i] - T * a[i]
            o = a[i] + T * shifted[i]
            row.append(jnp.where(self.even, e, turn(o, 1)))
            row.append(jnp.where(self.even, turn(e, -1), o))
        if len(a) > 1 and with_edge:
            e = shifted[-1] - T * a[-1]
            o = a[-1] + T * shifted[-1]
            row.append(jnp.where(self.even, e, turn(o, 1)))
        return row

    def synthesize(self, low, high, with_edge=True):
        a = [i - Q * j for i, j in zip(low, high)]
        b = [j + Q * i for i, j in zip(low, high)]
        return self.join(a, b, with_edge)


def plus(x, y, scale=1.0):
    return [i + (j if scale == 1.0 else scale * j) for i, j in zip(x, y)]


def times(scale, x):
    return [scale * i for i in x]


def mul(x, y):
    return [i * j for i, j in zip(x, y)]


def pair(x0, x1):
    return plus(x1, x0, -T), plus(x0, x1, T)


def unpair(a, b):
    return plus(b, a, -T), plus(a, b, T)


def read_row(x_refs, left_ref, right_ref, lon, lons, k):
    row = [x_ref[pl.ds(lon, SUB, stride=lons), :] for x_ref in x_refs]
    group, within = divmod(lon, lons // 4)
    beyond = turn(right_ref[pl.ds(within, SUB, stride=lons // 4), :], -HALO * group)
    before = turn(left_ref[pl.ds(within, SUB, stride=lons // 4), :], LANES - HALO - HALO * group)
    row.append(jnp.where(k.l < LANES // 2, beyond, before))
    return row


def put(ref, at, values):
    for i, v in enumerate(values):
        ref[:, pl.ds(LANES * (at + i), LANES)] = v


def get(ref, at, count):
    return [ref[:, pl.ds(LANES * (at + i), LANES)] for i in range(count)]


def edges_kernel(lons, members, first_ref, last_ref, table_ref, left_ref, right_ref):
    l = lane()
    groups = lons // 4
    for block in range(members // SUB):
        for within in range(groups):
            to_left = to_right = None
            for group in range(4):
                rows = pl.ds(SUB * lons * block + groups * group + within, SUB, stride=lons)
                here = (l >> 5) == group
                a = turn(first_ref[rows, :], HALO * group)
                b = turn(last_ref[rows, :], HALO * group - (LANES - HALO))
                to_left = a if to_left is None else jnp.where(here, a, to_left)
                to_right = b if to_right is None else jnp.where(here, b, to_right)
            out = pl.ds(SUB * groups * block + within, SUB, stride=groups)
            left_ref[out, :] = to_left
            right_ref[out, :] = to_right
    right_ref[pl.ds(members * groups, SUB), :] = table_ref[...]


def weights_kernel(index_ref, table_ref, halo_ref, out_ref, arranged_ref):
    k = Lanes()
    row = get(table_ref, 0, table_ref.shape[1] // LANES)
    row.append(jnp.where(k.l >= LANES - 16, halo_ref[...], 0.0))
    for level in range(LEVELS):
        if level == LEVELS - 1:
            values = [jnp.where(k.even, row[0], turn(row[1], 1))]
        else:
            values = k.unsorted(row) if len(row) > 2 else [pick(row[0], k.unsort), pick(row[1], k.unsort_edge)]
        scale = tap_1 ** (4 * (level + 1))
        for i, v in enumerate(values):
            arranged_ref[i] = v * scale
        for band in range(3 if level < LEVELS - 1 else 4):
            table_row = index_ref[3 * level + band]
            for i in range(len(values)):
                out_ref[WEIGHTS[level, band] + i] = jnp.broadcast_to(
                    arranged_ref[i, pl.ds(table_row, 1), :], (SUB, LANES)
                )
        if level < LEVELS - 2:
            pairs = [jnp.where(k.even, row[i], turn(row[i + 1], 1)) for i in range(0, len(row) - 1, 2)]
            row = [pick(v, k.sort) for v in pairs] + [
                jnp.where(k.l >= LANES // 2, pick(row[-1], k.sort_edge), 0.0)
            ]


def send_kernel(lons, x_refs, left_ref, right_ref, c1_ref, to_right, to_left, far_right, far_left):
    k = Lanes()
    half = lons // 2
    edge_right = edge_left = jnp.zeros((SUB, LANES), jnp.float32)

    def window(item):
        start = {"h": 112, "c1": 112, "b1": 112, "a1": 112, "a2": 120, "b2": 120, "k": 124, "b3": 124, "g": 126}[item]
        width = {"h": 32, "c1": 32, "b1": 32, "a1": 32, "a2": 16, "b2": 16, "k": 8, "b3": 8, "g": 1}[item]
        return ((k.l - (start + TURN[item])) & 127) < width

    def fill(edge, item, value):
        return jnp.where(window(item), turn(value, TURN[item]), edge)

    c1 = [None] * half
    b_next = None
    for i in reversed(range(half)):
        a, b = pair(
            read_row(x_refs, left_ref, right_ref, 2 * i, lons, k),
            read_row(x_refs, left_ref, right_ref, 2 * i + 1, lons, k),
        )
        if i == half - 1:
            h, g = k.analyze(a)
            h = k.sorted(h)
            put(to_right, RIGHT["h"], h[:-1])
            put(to_right, RIGHT["g"], g[:-1])
            edge_right = fill(edge_right, "h", h[-1])
            edge_right = fill(edge_right, "g", g[-1])
            c1[i] = h
        else:
            c1[i] = k.sorted(k.low(plus(a, b_next, Q)))
            put(c1_ref, 5 * i, c1[i])
        if i == 0:
            h, g = k.analyze(b)
            h0b = k.sorted(h)
            put(to_left, LEFT["h"], h0b[:-1])
            put(to_left, LEFT["g"], g[:-1])
            edge_left = fill(edge_left, "h", h0b[-1])
            edge_left = fill(edge_left, "g", g[-1])
        b_next = b
    put(to_right, RIGHT["c1"], c1[half - 2][:-1])
    edge_right = fill(edge_right, "c1", c1[half - 2][-1])

    pairs1 = [pair(c1[2 * i], c1[2 * i + 1]) for i in range(half // 2)]
    a1 = pairs1[-2][0]
    put(to_right, RIGHT["a1"], a1[:-1])
    edge_right = fill(edge_right, "a1", a1[-1])
    b1 = pairs1[0][1]
    put(to_left, LEFT["b1"], b1[:-1])
    edge_left = fill(edge_left, "b1", b1[-1])

    def lows(pairs):
        rows = [plus(pairs[i][0], pairs[i + 1][1], Q) for i in range(len(pairs) - 1)] + [pairs[-1][0]]
        return [k.sorted(k.low(row)) for row in rows]

    c2 = lows(pairs1)
    pairs2 = [pair(c2[2 * i], c2[2 * i + 1]) for i in range(half // 4)]
    a2 = pairs2[-2][0]
    put(to_right, RIGHT["a2"], a2[:-1])
    edge_right = fill(edge_right, "a2", a2[-1])
    b2 = pairs2[0][1]
    put(to_left, LEFT["b2"], b2[:-1])
    edge_left = fill(edge_left, "b2", b2[-1])
    c3 = lows(pairs2)
    a3, b3 = pair(c3[0], c3[1])
    put(far_right, 0, a3)
    put(to_left, LEFT["b3"], b3[:-1])
    edge_left = fill(edge_left, "b3", b3[-1])

    d1 = times(Q, h0b)
    d2 = [k.sorted(k.low(times(Q * T, d1))), k.sorted(k.low(plus(d1, b1, Q)))]
    da, db = pair(d2[0], d2[1])
    d3 = [k.sorted(k.low(times(Q, db))), k.sorted(k.low(plus(da, b2, Q)))]
    ka, kb = pair(d3[0], d3[1])
    put(to_right, RIGHT["k"], ka[:-1])
    edge_right = fill(edge_right, "k", ka[-1])
    put(far_left, 0, kb)
    put(to_right, RIGHT["edge"], [edge_right])
    put(to_left, LEFT["edge"], [edge_left])


def inner_kernel(lons, w_ref, x_refs, left_ref, right_ref, out_ref):
    k = Lanes()
    half = lons // 2

    def weight(band):
        return [w_ref[WEIGHTS[0, band] + i] for i in range(5)]

    def store(p, a, b):
        y0, y1 = unpair(a, b)
        put(out_ref, 2 * p * len(a), y0)
        put(out_ref, (2 * p + 1) * len(a), y1)

    def rows(i):
        return pair(
            read_row(x_refs, left_ref, right_ref, 2 * i, lons, k),
            read_row(x_refs, left_ref, right_ref, 2 * i + 1, lons, k),
        )

    a, b = rows(0)
    before = [jnp.zeros((SUB, LANES), jnp.float32)] * (len(a) - 1)
    for p in range(half):
        if p == half - 1:
            store(p, [jnp.zeros((SUB, LANES), jnp.float32)] * len(before), before)
            break
        a_next, b_next = rows(p + 1)
        low = plus(a, b_next, Q)
        high = plus(b_next, a, -Q)
        hh, hg = k.analyze(high)
        z = k.synthesize(mul(hh, weight(1)), mul(hg, weight(2)), False)
        _, lg = k.analyze(low)
        lg = mul(lg, weight(0))
        y = k.join(times(-Q, lg), lg, False)
        store(p, plus(y, z, -Q), before)
        before = plus(z, y, Q)
        a, b = a_next, b_next


def outer_kernel(
    lons, w_ref, part_ref, c1_ref, own_right, own_left, from_left, from_right, far_left, far_right, out_ref, y_ref
):
    k = Lanes()
    half = lons // 2

    def item(ref, name, places):
        edge = turn(get(ref, places["edge"], 1)[0], -TURN[name])
        return get(ref, places[name], COUNT[name]) + [edge]

    def weight(level, band):
        return [w_ref[WEIGHTS[level, band] + i] for i in range((5, 3, 2, 1)[level])]

    ha, ga = item(own_right, "h", RIGHT), item(own_right, "g", RIGHT)
    hb, gb = item(own_left, "h", LEFT), item(own_left, "g", LEFT)
    ha_before, ga_before = item(from_left, "h", RIGHT), item(from_left, "g", RIGHT)
    hb_beyond, gb_beyond = item(from_right, "h", LEFT), item(from_right, "g", LEFT)

    def inner(level, rows, a_first, b_last):
        pairs = [pair(rows[2 * i], rows[2 * i + 1]) for i in range(len(rows) // 2)]
        a = [a_first] + [p[0] for p in pairs]
        b = [p[1] for p in pairs] + [b_last]
        coarse, band_0, highs = [], [], []
        for i in range(len(a)):
            low = plus(a[i], b[i], Q)
            high = plus(b[i], a[i], -Q)
            h, g = k.analyze(high)
            highs.append(k.synthesize(mul(h, weight(level, 1)), mul(g, weight(level, 2))))
            h, g = k.analyze(low)
            coarse.append(h if level == LEVELS - 1 else k.sorted(h))
            band_0.append(mul(g, weight(level, 0)))
        return coarse, band_0, highs

    def outer(lows, highs):
        a = [plus(l, h, -Q) for l, h in zip(lows, highs)]
        b = [plus(h, l, Q) for l, h in zip(lows, highs)]
        rows = []
        for i in range(1, len(a)):
            rows.extend(unpair(a[i], b[i - 1]))
        return rows

    c1 = [item(from_left, "c1", RIGHT), plus(ha_before, hb, Q)]
    c1 += [get(c1_ref, 5 * i, 5) for i in range(half - 1)]
    c1.append(plus(ha, hb_beyond, Q))
    c2, g1, z1 = inner(1, c1, item(from_left, "a1", RIGHT), item(from_right, "b1", LEFT))
    c3, g2, z2 = inner(2, c2, item(from_left, "a2", RIGHT), item(from_right, "b2", LEFT))
    a3 = plus(get(far_left, 0, 2), item(from_left, "k", RIGHT))
    b3 = plus(item(from_right, "b3", LEFT), get(far_right, 0, 2))
    c4, g3, z3 = inner(3, c3, a3, b3)
    lows = [k.synthesize(mul(c, weight(3, 3)), g) for c, g in zip(c4, g3)]
    field = outer(lows, z3)
    for g_rows, z_rows in ((g2, z2), (g1, z1)):
        unsort = (
            lambda row: [pick(row[0], k.unsort), pick(row[1], k.unsort_edge)] if len(row) == 2 else k.unsorted(row)
        )
        lows = [k.synthesize(unsort(f), g) for f, g in zip(field, g_rows)]
        field = outer(lows, z_rows)
    field = field[1:]

    def high_row(h, g):
        return k.synthesize(mul(k.unsorted(h), weight(0, 1)), mul(g, weight(0, 2)), False)

    def low_row(f, g=None):
        f = k.unsorted(f)
        if g is None:
            return k.join(f, times(Q, f), False)
        return k.synthesize(f, mul(g, weight(0, 0)), False)

    low = low_row(field[0], plus(ga_before, gb, Q))
    high = high_row(plus(hb, ha_before, -Q), plus(gb, ga_before, -Q))
    b = plus(high, low, Q)
    for p in range(half):
        if p < half - 1:
            a = low_row(field[p + 1])
            b_next = times(Q, a)
        else:
            low = low_row(field[p + 1], plus(ga, gb_beyond, Q))
            high = high_row(plus(hb_beyond, ha, -Q), plus(gb_beyond, ga, -Q))
            a = plus(low, high, -Q)
            b_next = None
        for j, y in enumerate(unpair(a, b)):
            part = get(part_ref, (2 * p + j) * len(y), len(y))
            for v in range(len(y)):
                y_ref[v, pl.ds(2 * p + j, SUB, stride=lons), :] = part[v] + y[v]
        b = b_next
    for v in range(y_ref.shape[0]):
        out_ref[:, pl.ds(LANES * v, LANES)] = y_ref[v]


def shift(x, axis, by, cyclic):
    size = lax.axis_size(axis)
    if cyclic:
        pairs = [(i, (i + by) % size) for i in range(size)]
    else:
        pairs = [(i, i + by) for i in range(size) if 0 <= i + by < size]
    return lax.ppermute(x, axis, pairs)


def per_device(perturbation, weight_table, band_index):
    members, lons, lats = perturbation.shape
    assert lons == 16 and lats == 8 * LANES and members % SUB == 0
    steps = members // SUB
    x = perturbation.reshape(members * lons, lats)
    shape = lambda *dims: jax.ShapeDtypeStruct(dims, jnp.float32)
    groups = lons // 4
    edge_rows = members * groups
    params = pltpu.CompilerParams(vmem_limit_bytes=60 * 1024 * 1024)

    to_left, to_right = pl.pallas_call(
        lambda *refs: edges_kernel(lons, members, *refs),
        grid=(1,),
        in_specs=[
            pl.BlockSpec((members * lons, LANES), lambda i: (0, 0)),
            pl.BlockSpec((members * lons, LANES), lambda i: (0, lats // LANES - 1)),
            pl.BlockSpec((8, LANES), lambda i: (0, lats // 2 // LANES - 1)),
        ],
        out_specs=[
            pl.BlockSpec((edge_rows, LANES), lambda i: (0, 0)),
            pl.BlockSpec((edge_rows + 8, LANES), lambda i: (0, 0)),
        ],
        out_shape=[shape(edge_rows, LANES), shape(edge_rows + 8, LANES)],
        compiler_params=params,
        name="edges",
    )(x, x, weight_table)
    before = shift(to_right, "lat", 1, False)
    beyond = shift(to_left, "lat", -1, False)

    weights = pl.pallas_call(
        weights_kernel,
        grid=(1,),
        in_specs=[
            pl.BlockSpec(memory_space=pltpu.SMEM),
            pl.BlockSpec((8, lats // 2), lambda i: (0, 0)),
            pl.BlockSpec((8, LANES), lambda i: (edge_rows // 8, 0)),
        ],
        out_specs=pl.BlockSpec((WEIGHT_COUNT, SUB, LANES), lambda i: (0, 0, 0)),
        out_shape=shape(WEIGHT_COUNT, SUB, LANES),
        scratch_shapes=[pltpu.VMEM((5, SUB, LANES), jnp.float32)],
        compiler_params=params,
        name="weights",
    )(band_index, weight_table, before)

    by_member = lambda width: pl.BlockSpec((SUB, width), lambda i: (i, 0))
    x_spec = pl.BlockSpec((SUB * lons, lats), lambda i: (i, 0))
    cols = lats // LANES
    x_specs = [pl.BlockSpec((SUB * lons, LANES), lambda i, v=v: (i, v)) for v in range(cols)]
    halo_spec = pl.BlockSpec((SUB * groups, LANES), lambda i: (i, 0))
    w_spec = pl.BlockSpec((WEIGHT_COUNT, SUB, LANES), lambda i: (0, 0, 0))
    c1_width = (lons // 2 - 1) * 5 * LANES
    right_width, left_width = RIGHT_SIZE * LANES, LEFT_SIZE * LANES
    c1, to_right, to_left, far_right, far_left = pl.pallas_call(
        lambda *refs: send_kernel(lons, refs[:cols], *refs[cols:]),
        grid=(steps,),
        in_specs=x_specs + [halo_spec, halo_spec],
        out_specs=[by_member(c1_width), by_member(right_width), by_member(left_width)] + [by_member(2 * LANES)] * 2,
        out_shape=[
            shape(members, c1_width),
            shape(members, right_width),
            shape(members, left_width),
            shape(members, 2 * LANES),
            shape(members, 2 * LANES),
        ],
        compiler_params=params,
        cost_estimate=pl.CostEstimate(flops=10**7, bytes_accessed=10**7, transcendentals=0),
        name="send",
    )(*[x] * cols, before, beyond)
    from_left = shift(to_right, "lon", 1, True)
    from_right = shift(to_left, "lon", -1, True)
    from_far_left = shift(far_right, "lon", 2, True)
    from_far_right = shift(far_left, "lon", -2, True)

    part = pl.pallas_call(
        lambda *refs: inner_kernel(lons, refs[0], refs[1 : cols + 1], *refs[cols + 1 :]),
        grid=(steps,),
        in_specs=[w_spec] + x_specs + [halo_spec, halo_spec],
        out_specs=by_member(lons * lats),
        out_shape=shape(members, lons * lats),
        compiler_params=params,
        cost_estimate=pl.CostEstimate(flops=10**7, bytes_accessed=4 * 10**7, transcendentals=0),
        name="inner",
    )(weights, *[x] * cols, before, beyond)

    out = pl.pallas_call(
        lambda *refs: outer_kernel(lons, *refs),
        grid=(steps,),
        in_specs=[w_spec, by_member(lons * lats), by_member(c1_width), by_member(right_width), by_member(left_width)]
        + [by_member(right_width), by_member(left_width)]
        + [by_member(2 * LANES)] * 2,
        out_specs=x_spec,
        out_shape=shape(members * lons, lats),
        scratch_shapes=[pltpu.VMEM((cols, SUB * lons, LANES), jnp.float32)],
        compiler_params=params,
        name="outer",
    )(weights, part, c1, to_right, to_left, from_left, from_right, from_far_left, from_far_right)
    return out.reshape(members, lons, lats)


def solution(mesh):
    placed = (P(None, "lon", "lat"), P(None, "lat"), P())
    return jax.shard_map(
        per_device, mesh=mesh, in_specs=placed, out_specs=P(None, "lon", "lat"), check_vma=False
    )
```

```python
import math

import jax
import jax.numpy as jnp
from jax import lax
from jax.experimental import pallas as pl
from jax.experimental.pallas import tpu as pltpu
from jax.sharding import PartitionSpec as P

LEVELS = 4
LANES = 128
SUB = 8
BLOCK = 8
HALO = 32

root_three = math.sqrt(3.0)
tap_0 = (1.0 + root_three) / (4.0 * math.sqrt(2.0))
tap_1 = (3.0 + root_three) / (4.0 * math.sqrt(2.0))
tap_2 = (3.0 - root_three) / (4.0 * math.sqrt(2.0))
tap_3 = (1.0 - root_three) / (4.0 * math.sqrt(2.0))
T = tap_3 / tap_2
Q = tap_2 / tap_1


RIGHT = {"c1": 0, "a1": 4, "a2": 8, "k": 10, "edge": 11}
LEFT = {"b1": 0, "b2": 4, "b3": 6, "edge": 7}
RIGHT_SIZE = 13
LEFT_SIZE = 8
EDGE = {
    "c1": (0, 0, 2),
    "a1": (0, 1, 2),
    "a0": (0, 64, 1),
    "a2": (1, 0, 4),
    "k": (1, 1, 8),
    "b1": (0, 0, 2),
    "b2": (0, 1, 4),
    "b3": (0, 3, 8),
    "b0": (0, 64, 1),
}
COUNT = {"c1": 4, "a1": 4, "b1": 4, "a2": 2, "b2": 2, "k": 1, "b3": 1}
MAINS = (4, 2, 1, 1)
WEIGHTS = {}
WEIGHT_COUNT = 0
for level_at in range(LEVELS):
    for band_at in range(3 if level_at < LEVELS - 1 else 4):
        WEIGHTS[level_at, band_at] = WEIGHT_COUNT
        WEIGHT_COUNT += MAINS[level_at] + 1


def turn(v, by):
    by = by % LANES
    return v if by == 0 else pltpu.roll(v, by, 1)


def pick(v, index):
    return jnp.take_along_axis(v, index, axis=1, mode="promise_in_bounds")


class Lanes:
    def __init__(self, rows):
        l = lax.broadcasted_iota(jnp.int32, (rows, LANES), 1)
        self.l = l
        self.zero = jnp.zeros((rows, LANES), jnp.float32)
        self.bit = [(l & (1 << level)) == 0 for level in range(LEVELS)]

    def split(self, row, level):
        main, edge = row[:-1], row[-1]
        d, stride, bit = 1 << level, 2 << level, self.bit[level]
        half = len(main) // 2
        evens = [jnp.where(bit, main[j], turn(main[j + half], d)) for j in range(half)] or [main[0]]
        odds = [jnp.where(bit, turn(main[j], -d), main[j + half]) for j in range(half)] or [turn(main[0], -d)]
        evens.append(edge)
        odds.append(turn(edge, -d))
        a = [o - T * e for e, o in zip(evens, odds)]
        b = [e + T * o for e, o in zip(evens, odds)]
        n = len(b) - 1
        shifted = [turn(jnp.where(self.l < stride, b[j + 1], b[j]), -stride) for j in range(n - 1)]
        l, first, beyond = self.l, b[0], b[-1]
        if level == 0:
            m = jnp.where(l == 0, turn(first, -1), jnp.where(l == 1, turn(beyond, 1), b[n - 1]))
        elif level == 1:
            m = jnp.where(l == 2, turn(first, 1), jnp.where(l == 3, turn(beyond, 3), b[n - 1]))
            m = jnp.where(l < 2, turn(first, -2), m)
        else:
            m = jnp.where(l == 6, turn(first, 5), jnp.where(l == 7, turn(beyond, 7), b[n - 1]))
            m = jnp.where(l < 4, turn(first, -4), jnp.where(l < 6, turn(first, 2), m))
            m = jnp.where(l < 8, m, b[n - 1])
        shifted.append(turn(m, -stride))
        shifted.append(turn(jnp.where(l == 0, first, beyond), -stride))
        return a, shifted

    def analyze(self, row, level):
        a, b = self.split(row, level)
        return [i + Q * j for i, j in zip(a, b)], [j - Q * i for i, j in zip(a, b)]

    def low(self, row, level):
        a, b = self.split(row, level)
        return [i + Q * j for i, j in zip(a, b)]

    def join(self, a, b, level):
        d, stride, bit = 1 << level, 2 << level, self.bit[level]
        with_edge = level > 0
        n = len(b) - 1
        l, last, before = self.l, b[n - 1], b[-1]
        x = l - (LANES - stride)
        if level == 0:
            m = jnp.where(x == 0, before, jnp.where(x == 1, turn(last, 1), b[0]))
        elif level == 1:
            m = jnp.where(x == 0, before, jnp.where(x == 1, turn(last, -1), jnp.where(x >= 2, turn(last, 2), b[0])))
        else:
            m = jnp.where(x == 0, before, jnp.where(x == 1, turn(last, -5), b[0]))
            m = jnp.where(x >= 4, turn(last, 4), jnp.where(x >= 2, turn(last, -2), m))
        shifted = [turn(m, stride)]
        shifted += [turn(jnp.where(x >= 0, b[j - 1], b[j]), stride) for j in range(1, n)]
        evens = [s - T * i for i, s in zip(a, shifted)]
        odds = [i + T * s for i, s in zip(a, shifted)]
        row = [jnp.where(bit, e, turn(o, d)) for e, o in zip(evens, odds)]
        if level < LEVELS - 1:
            row += [jnp.where(bit, turn(e, -d), o) for e, o in zip(evens, odds)]
        if with_edge:
            s = turn(b[-1], stride)
            row.append(jnp.where(bit, s - T * a[-1], turn(a[-1] + T * s, d)))
        return row

    def synthesize(self, low, high, level):
        a = [i - Q * j for i, j in zip(low, high)]
        b = [j + Q * i for i, j in zip(low, high)]
        return self.join(a, b, level)

    def fill(self, edges, item, value):
        at, by, every = EDGE[item]
        l = (self.l - by) & (LANES - 1)
        here = (((l - 64 - HALO) & (LANES - 1)) < 64) & ((l & (every - 1)) == 0)
        edges[at] = jnp.where(here, turn(value, by), edges[at])


def plus(x, y, scale=1.0):
    return [i + (j if scale == 1.0 else scale * j) for i, j in zip(x, y)]


def times(scale, x):
    return [scale * i for i in x]


def mul(x, y):
    return [i * j for i, j in zip(x, y)]


def pair(x0, x1):
    return plus(x1, x0, -T), plus(x0, x1, T)


def unpair(a, b):
    return plus(b, a, -T), plus(a, b, T)


def read_row(x_refs, left_ref, right_ref, lon, lons, k):
    rows = k.l.shape[0]
    row = [x_ref[pl.ds(lon, rows, stride=lons), :] for x_ref in x_refs]
    group, within = divmod(lon, lons // 4)
    beyond = turn(right_ref[within], -HALO * group)
    before = turn(left_ref[within], LANES - HALO - HALO * group)
    row.append(jnp.where(k.l < LANES // 2, beyond, before))
    return row


def put(ref, at, values):
    for i, v in enumerate(values):
        ref[:, pl.ds(LANES * (at + i), LANES)] = v


def get(ref, at, count):
    return [ref[:, pl.ds(LANES * (at + i), LANES)] for i in range(count)]


def first_kernel(lons, block, x_refs, table_ref, to_left_ref, to_right_ref, a_ref, b_ref):
    k = Lanes(block)
    groups = lons // 4

    def row(lon):
        return [x_ref[pl.ds(lon, block, stride=lons), :] for x_ref in x_refs]

    put(b_ref, 0, pair(row(0), row(1))[1])
    put(a_ref, 0, pair(row(lons - 2), row(lons - 1))[0])
    at = pl.ds(pl.multiple_of(pl.program_id(0) * block, block), block)
    for within in range(groups):
        to_left = to_right = None
        for group in range(4):
            lon = groups * group + within
            here = (k.l >> 5) == group
            a = turn(x_refs[0][pl.ds(lon, block, stride=lons), :], HALO * group)
            b = turn(x_refs[-1][pl.ds(lon, block, stride=lons), :], HALO * group - (LANES - HALO))
            to_left = a if to_left is None else jnp.where(here, a, to_left)
            to_right = b if to_right is None else jnp.where(here, b, to_right)
        to_left_ref[within] = to_left
        to_right_ref[within, at, :] = to_right

    @pl.when(pl.program_id(0) == 0)
    def _():
        members = to_right_ref.shape[1] - SUB
        for within in range(groups):
            to_right_ref[within, pl.ds(members, SUB), :] = table_ref[...]


def weights_kernel(index_ref, table_ref, halo_ref, out_ref, arranged_ref):
    l = lax.broadcasted_iota(jnp.int32, (SUB, LANES), 1)
    block = out_ref.shape[1]
    table = get(table_ref, 0, table_ref.shape[1] // LANES)
    halo = jnp.where(l >= LANES - 16, halo_ref[0], 0.0)
    for level in range(LEVELS):
        scale = tap_1 ** (4 * (level + 1))
        mains = MAINS[level]
        stride = 2 << level
        count = 64 * len(table) >> level
        step = LANES // stride
        start, size = 0 * l, count * 2
        for bit in range(min(level + 1, 3)):
            size = size // 2
            start = start + size * ((l >> bit) & 1)
        for j in range(mains):
            k = (start + step * j + l // stride) << level
            value = jnp.zeros((SUB, LANES), jnp.float32)
            for v in range(len(table)):
                value = jnp.where((k >> 7) == v, pick(table[v], k & 127), value)
            arranged_ref[j] = value * scale
        edge = pick(halo, 64 + (l >> 1))
        arranged_ref[mains] = jnp.where(l >= LANES - 2 * stride, edge, 0.0) * scale
        for band in range(3 if level < LEVELS - 1 else 4):
            table_row = index_ref[3 * level + band]
            for i in range(mains + 1):
                out_ref[WEIGHTS[level, band] + i] = jnp.broadcast_to(
                    arranged_ref[i, pl.ds(table_row, 1), :], (block, LANES)
                )


def send_kernel(lons, block, x_refs, left_ref, right_ref, c1_ref, to_right, to_left, far_right, far_left):
    k = Lanes(block)
    half = lons // 2
    edges_right, edges_left = [k.zero, k.zero], [k.zero]

    c1 = [None] * half
    b_next = None
    for i in reversed(range(half)):
        a, b = pair(
            read_row(x_refs, left_ref, right_ref, 2 * i, lons, k),
            read_row(x_refs, left_ref, right_ref, 2 * i + 1, lons, k),
        )
        if i == half - 1:
            k.fill(edges_right, "a0", a[-1])
            c1[i] = k.low(a, 0)
        else:
            c1[i] = k.low(plus(a, b_next, Q), 0)
            put(c1_ref, 5 * i, c1[i])
        if i == 0:
            k.fill(edges_left, "b0", b[-1])
            h0b = k.low(b, 0)
        b_next = b

    def message(ref, places, edges, item, row):
        put(ref, places[item], row[:-1])
        k.fill(edges, item, row[-1])

    message(to_right, RIGHT, edges_right, "c1", c1[half - 2])
    pairs1 = [pair(c1[2 * i], c1[2 * i + 1]) for i in range(half // 2)]
    message(to_right, RIGHT, edges_right, "a1", pairs1[-2][0])
    b1 = pairs1[0][1]
    message(to_left, LEFT, edges_left, "b1", b1)

    def lows(pairs, level):
        rows = [plus(pairs[i][0], pairs[i + 1][1], Q) for i in range(len(pairs) - 1)] + [pairs[-1][0]]
        return [k.low(row, level) for row in rows]

    c2 = lows(pairs1, 1)
    pairs2 = [pair(c2[2 * i], c2[2 * i + 1]) for i in range(half // 4)]
    message(to_right, RIGHT, edges_right, "a2", pairs2[-2][0])
    b2 = pairs2[0][1]
    message(to_left, LEFT, edges_left, "b2", b2)
    c3 = lows(pairs2, 2)
    a3, b3 = pair(c3[0], c3[1])
    put(far_right, 0, a3)
    message(to_left, LEFT, edges_left, "b3", b3)

    d1 = times(Q, h0b)
    d2 = [k.low(times(Q * T, d1), 1), k.low(plus(d1, b1, Q), 1)]
    da, db = pair(d2[0], d2[1])
    d3 = [k.low(times(Q, db), 2), k.low(plus(da, b2, Q), 2)]
    ka, kb = pair(d3[0], d3[1])
    message(to_right, RIGHT, edges_right, "k", ka)
    put(far_left, 0, kb)
    put(to_right, RIGHT["edge"], edges_right)
    put(to_left, LEFT["edge"], edges_left)


def inner_kernel(lons, block, w_ref, x_refs, left_ref, right_ref, out_ref):
    k = Lanes(block)
    half = lons // 2

    def weight(band):
        return [w_ref[WEIGHTS[0, band] + i] for i in range(5)]

    def store(p, a, b):
        y0, y1 = unpair(a, b)
        put(out_ref, 2 * p * len(a), y0)
        put(out_ref, (2 * p + 1) * len(a), y1)

    def rows(i):
        return pair(
            read_row(x_refs, left_ref, right_ref, 2 * i, lons, k),
            read_row(x_refs, left_ref, right_ref, 2 * i + 1, lons, k),
        )

    a, b = rows(0)
    before = [k.zero] * (len(a) - 1)
    for p in range(half):
        if p == half - 1:
            store(p, [k.zero] * len(before), before)
            break
        a_next, b_next = rows(p + 1)
        low = plus(a, b_next, Q)
        high = plus(b_next, a, -Q)
        hh, hg = k.analyze(high, 0)
        z = k.synthesize(mul(hh, weight(1)), mul(hg, weight(2)), 0)
        _, lg = k.analyze(low, 0)
        lg = mul(lg, weight(0))
        y = k.join(times(-Q, lg), lg, 0)
        store(p, plus(y, z, -Q), before)
        before = plus(z, y, Q)
        a, b = a_next, b_next


def outer_kernel(
    lons,
    block,
    w_ref,
    part_ref,
    c1_ref,
    own_a,
    own_b,
    own_right,
    own_left,
    left_a,
    right_b,
    from_left,
    from_right,
    far_left,
    far_right,
    out_ref,
    y_ref,
):
    k = Lanes(block)
    half = lons // 2

    def edge(ref, name, places):
        at, by, _ = EDGE[name]
        return turn(get(ref, places["edge"] + at, 1)[0], -by)

    def item(ref, name, places):
        return get(ref, places[name], COUNT[name]) + [edge(ref, name, places)]

    def weight(level, band):
        return [w_ref[WEIGHTS[level, band] + i] for i in range(MAINS[level] + 1)]

    def inner(level, rows, a_first, b_last):
        pairs = [pair(rows[2 * i], rows[2 * i + 1]) for i in range(len(rows) // 2)]
        a = [a_first] + [p[0] for p in pairs]
        b = [p[1] for p in pairs] + [b_last]
        coarse, band_0, highs = [], [], []
        for i in range(len(a)):
            h, g = k.analyze(plus(b[i], a[i], -Q), level)
            highs.append(k.synthesize(mul(h, weight(level, 1)), mul(g, weight(level, 2)), level))
            h, g = k.analyze(plus(a[i], b[i], Q), level)
            coarse.append(h)
            band_0.append(mul(g, weight(level, 0)))
        return coarse, band_0, highs

    def outer(lows, highs):
        a = [plus(l, h, -Q) for l, h in zip(lows, highs)]
        b = [plus(h, l, Q) for l, h in zip(lows, highs)]
        rows = []
        for i in range(1, len(a)):
            rows.extend(unpair(a[i], b[i - 1]))
        return rows

    def straddling(a, b):
        c, g = k.analyze(plus(a, b, Q), 0)
        h1, h2 = k.analyze(plus(b, a, -Q), 0)
        return c, mul(g, weight(0, 0)), k.synthesize(mul(h1, weight(0, 1)), mul(h2, weight(0, 2)), 0)

    count = own_a.shape[1] // LANES
    c_first, g_first, z_first = straddling(
        get(left_a, 0, count) + [edge(from_left, "a0", RIGHT)],
        get(own_b, 0, count) + [edge(own_left, "b0", LEFT)],
    )
    c_last, g_last, z_last = straddling(
        get(own_a, 0, count) + [edge(own_right, "a0", RIGHT)],
        get(right_b, 0, count) + [edge(from_right, "b0", LEFT)],
    )

    c1 = [item(from_left, "c1", RIGHT), c_first]
    c1 += [get(c1_ref, 5 * i, 5) for i in range(half - 1)]
    c1.append(c_last)
    c2, g1, z1 = inner(1, c1, item(from_left, "a1", RIGHT), item(from_right, "b1", LEFT))
    c3, g2, z2 = inner(2, c2, item(from_left, "a2", RIGHT), item(from_right, "b2", LEFT))
    a3 = plus(get(far_left, 0, 2), item(from_left, "k", RIGHT))
    b3 = plus(item(from_right, "b3", LEFT), get(far_right, 0, 2))
    c4, g3, z3 = inner(3, c3, a3, b3)
    field = [mul(c, weight(3, 3)) for c in c4]
    for level, g_rows, z_rows in ((3, g3, z3), (2, g2, z2), (1, g1, z1)):
        field = outer([k.synthesize(f, g, level) for f, g in zip(field, g_rows)], z_rows)
    field = field[1:]

    low = k.synthesize(field[0], g_first, 0)
    b = plus(z_first, low, Q)
    for p in range(half):
        if p < half - 1:
            f = field[p + 1]
            a = k.join(f, times(Q, f), 0)
            b_next = times(Q, a)
        else:
            low = k.synthesize(field[p + 1], g_last, 0)
            a = plus(low, z_last, -Q)
        for j, y in enumerate(unpair(a, b)):
            part = get(part_ref, (2 * p + j) * len(y), len(y))
            for v in range(len(y)):
                y_ref[v, pl.ds(block * (2 * p + j), block), :] = part[v] + y[v]
        b = b_next
    for v in range(y_ref.shape[0]):
        for member in range(block):
            out_ref[pl.ds(lons * member, lons), pl.ds(LANES * v, LANES)] = y_ref[
                v, pl.ds(member, lons, stride=block), :
            ]


def shift(x, axis, by, cyclic):
    size = lax.axis_size(axis)
    if cyclic:
        pairs = [(i, (i + by) % size) for i in range(size)]
    else:
        pairs = [(i, i + by) for i in range(size) if 0 <= i + by < size]
    return lax.ppermute(x, axis, pairs)


def per_device(perturbation, weight_table, band_index):
    members, lons, lats = perturbation.shape
    assert lons == 16 and lats == 8 * LANES and members % BLOCK == 0
    block = BLOCK
    steps = members // block
    x = perturbation.reshape(members * lons, lats)
    shape = lambda *dims: jax.ShapeDtypeStruct(dims, jnp.float32)
    groups = lons // 4
    cols = lats // LANES
    params = pltpu.CompilerParams(vmem_limit_bytes=60 * 1024 * 1024)
    by_member = lambda width: pl.BlockSpec((block, width), lambda i: (i, 0))
    x_specs = [pl.BlockSpec((block * lons, LANES), lambda i, v=v: (i, v)) for v in range(cols)]
    halo_spec = pl.BlockSpec((groups, block, LANES), lambda i: (0, i, 0))
    w_spec = pl.BlockSpec((WEIGHT_COUNT, block, LANES), lambda i: (0, 0, 0))

    to_left, to_right, own_a, own_b = pl.pallas_call(
        lambda *refs: first_kernel(lons, block, refs[:cols], *refs[cols:]),
        grid=(steps,),
        in_specs=x_specs + [pl.BlockSpec((SUB, LANES), lambda i: (0, lats // 2 // LANES - 1))],
        out_specs=[
            halo_spec,
            pl.BlockSpec((groups, members + SUB, LANES), lambda i: (0, 0, 0)),
            by_member(lats),
            by_member(lats),
        ],
        out_shape=[
            shape(groups, members, LANES),
            shape(groups, members + SUB, LANES),
            shape(members, lats),
            shape(members, lats),
        ],
        compiler_params=params,
        name="first",
    )(*[x] * cols, weight_table)
    before = shift(to_right, "lat", 1, False)
    beyond = shift(to_left, "lat", -1, False)
    left_a = shift(own_a, "lon", 1, True)
    right_b = shift(own_b, "lon", -1, True)

    weights = pl.pallas_call(
        weights_kernel,
        grid=(1,),
        in_specs=[
            pl.BlockSpec(memory_space=pltpu.SMEM),
            pl.BlockSpec((SUB, lats // 2), lambda i: (0, 0)),
            pl.BlockSpec((1, SUB, LANES), lambda i: (0, members // SUB, 0)),
        ],
        out_specs=pl.BlockSpec((WEIGHT_COUNT, block, LANES), lambda i: (0, 0, 0)),
        out_shape=shape(WEIGHT_COUNT, block, LANES),
        scratch_shapes=[pltpu.VMEM((5, SUB, LANES), jnp.float32)],
        compiler_params=params,
        name="weights",
    )(band_index, weight_table, before)

    c1_width = (lons // 2 - 1) * 5 * LANES
    right_width, left_width = RIGHT_SIZE * LANES, LEFT_SIZE * LANES
    c1, to_right, to_left, far_right, far_left = pl.pallas_call(
        lambda *refs: send_kernel(lons, block, refs[:cols], *refs[cols:]),
        grid=(steps,),
        in_specs=x_specs + [halo_spec, halo_spec],
        out_specs=[by_member(c1_width), by_member(right_width), by_member(left_width)] + [by_member(2 * LANES)] * 2,
        out_shape=[
            shape(members, c1_width),
            shape(members, right_width),
            shape(members, left_width),
            shape(members, 2 * LANES),
            shape(members, 2 * LANES),
        ],
        compiler_params=params,
        cost_estimate=pl.CostEstimate(flops=10**7, bytes_accessed=10**7, transcendentals=0),
        name="send",
    )(*[x] * cols, before, beyond)
    from_left = shift(to_right, "lon", 1, True)
    from_right = shift(to_left, "lon", -1, True)
    from_far_left = shift(far_right, "lon", 2, True)
    from_far_right = shift(far_left, "lon", -2, True)

    part = pl.pallas_call(
        lambda *refs: inner_kernel(lons, block, refs[0], refs[1 : cols + 1], *refs[cols + 1 :]),
        grid=(steps,),
        in_specs=[w_spec] + x_specs + [halo_spec, halo_spec],
        out_specs=by_member(lons * lats),
        out_shape=shape(members, lons * lats),
        compiler_params=params,
        cost_estimate=pl.CostEstimate(flops=10**7, bytes_accessed=4 * 10**7, transcendentals=0),
        name="inner",
    )(weights, *[x] * cols, before, beyond)

    out = pl.pallas_call(
        lambda *refs: outer_kernel(lons, block, *refs),
        grid=(steps,),
        in_specs=[w_spec, by_member(lons * lats), by_member(c1_width), by_member(lats), by_member(lats)]
        + [by_member(right_width), by_member(left_width), by_member(lats), by_member(lats)]
        + [by_member(right_width), by_member(left_width)]
        + [by_member(2 * LANES)] * 2,
        out_specs=pl.BlockSpec((block * lons, lats), lambda i: (i, 0)),
        out_shape=shape(members * lons, lats),
        scratch_shapes=[pltpu.VMEM((cols, block * lons, LANES), jnp.float32)],
        compiler_params=params,
        name="outer",
    )(
        weights,
        part,
        c1,
        own_a,
        own_b,
        to_right,
        to_left,
        left_a,
        right_b,
        from_left,
        from_right,
        from_far_left,
        from_far_right,
    )
    return out.reshape(members, lons, lats)


def solution(mesh):
    placed = (P(None, "lon", "lat"), P(None, "lat"), P())
    return jax.shard_map(
        per_device, mesh=mesh, in_specs=placed, out_specs=P(None, "lon", "lat"), check_vma=False
    )
```

```python
import math

import jax
import jax.numpy as jnp
from jax import lax
from jax.experimental import pallas as pl
from jax.experimental.pallas import tpu as pltpu
from jax.sharding import PartitionSpec as P


LEVELS = 4
LANES = 128
SUB = 8
BLOCK = 40
SEND_STACK = 4
INNER_STACK = 2
OUTER_STACK = 6
HALO = 32

root_three = math.sqrt(3.0)
tap_1 = (3.0 + root_three) / (4.0 * math.sqrt(2.0))
tap_2 = (3.0 - root_three) / (4.0 * math.sqrt(2.0))
tap_3 = (1.0 - root_three) / (4.0 * math.sqrt(2.0))
T = tap_3 / tap_2
Q = tap_2 / tap_1


RIGHT = {"c1": 0, "a1": 4, "a2": 8, "k": 10, "edge": 11}
LEFT = {"b1": 0, "b2": 4, "b3": 6, "edge": 7}
RIGHT_SIZE = 13
LEFT_SIZE = 8
EDGE = {
    "c1": (0, 0, 2),
    "a1": (0, 1, 2),
    "a0": (0, 64, 1),
    "a2": (1, 0, 4),
    "k": (1, 1, 8),
    "b1": (0, 0, 2),
    "b2": (0, 1, 4),
    "b3": (0, 3, 8),
    "b0": (0, 64, 1),
}
COUNT = {"c1": 4, "a1": 4, "b1": 4, "a2": 2, "b2": 2, "k": 1, "b3": 1}
MAINS = (4, 2, 1, 1)
WEIGHTS = {}
WEIGHT_COUNT = 0
for level_at in range(LEVELS):
    for band_at in range(3 if level_at < LEVELS - 1 else 4):
        WEIGHTS[level_at, band_at] = WEIGHT_COUNT
        WEIGHT_COUNT += MAINS[level_at] + 1


def turn(v, by):
    by = by % LANES
    return v if by == 0 else pltpu.roll(v, by, 1)


def pick(v, index):
    return jnp.take_along_axis(v, index, axis=1, mode="promise_in_bounds")


class Lanes:
    def __init__(self, rows):
        l = lax.broadcasted_iota(jnp.int32, (rows, LANES), 1)
        self.l = l
        self.zero = jnp.zeros((rows, LANES), jnp.float32)
        self.bit = [(l & (1 << level)) == 0 for level in range(LEVELS)]
        self.ahead, self.behind = [], []
        for level in range(LEVELS):
            stride = 2 << level
            bits = min(level + 1, 3)
            ahead, behind = (l + stride) & (LANES - 1), (l - stride) & (LANES - 1)
            flip = lambda x: int(format(x, "0%db" % bits)[::-1], 2)
            for x in range(1 << bits):
                after = flip((flip(x) + 1) % (1 << bits))
                ahead = jnp.where(l == LANES - stride + x, after, ahead)
                behind = jnp.where(l == after, LANES - stride + x, behind)
            self.ahead.append(ahead)
            self.behind.append(behind)

    def split(self, row, level):
        main, edge = row[:-1], row[-1]
        d, stride, bit, l = 1 << level, 2 << level, self.bit[level], self.l
        half = len(main) // 2
        right = [turn(main[j + half], d) for j in range(half)]
        left = [turn(main[j], -d) for j in range(half)] or [turn(main[0], -d)]
        left.append(turn(edge, -d))
        if half:
            evens = [jnp.where(bit, main[j], right[j]) for j in range(half)]
            odds = [jnp.where(bit, left[j], main[j + half]) for j in range(half)]
        else:
            evens, odds = [main[0]], [left[0]]
        evens.append(edge)
        odds.append(left[-1])
        a = [o - T * e for e, o in zip(evens, odds)]
        b = [e + T * o for e, o in zip(evens, odds)]
        n = len(b) - 1
        first, beyond = b[0], b[-1]
        shifted = [turn(jnp.where(l < stride, b[j + 1], b[j]), -stride) for j in range(n - 1)]
        m = jnp.where(l == 0, beyond, first)
        shifted.append(pick(m if n == 1 else jnp.where(l < stride, m, b[n - 1]), self.ahead[level]))
        shifted.append(turn(jnp.where(l == 0, first, beyond), -stride))
        return a, shifted

    def analyze(self, row, level):
        a, b = self.split(row, level)
        return [i + Q * j for i, j in zip(a, b)], [j - Q * i for i, j in zip(a, b)]

    def low(self, row, level):
        a, b = self.split(row, level)
        return [i + Q * j for i, j in zip(a, b)]

    def join(self, a, b, level):
        d, stride, bit, l = 1 << level, 2 << level, self.bit[level], self.l
        n = len(b) - 1
        top = l >= LANES - stride
        before = turn(b[-1], stride)
        m = b[0] if n == 1 else jnp.where(top, b[n - 1], b[0])
        shifted = [pick(m, self.behind[level])]
        shifted += [turn(jnp.where(top, b[j - 1], b[j]), stride) for j in range(1, n)]
        shifted[0] = jnp.where(l == 0, before, shifted[0])
        if level > 0:
            shifted.append(before)
        evens = [s - T * i for i, s in zip(a, shifted)]
        odds = [i + T * s for i, s in zip(a, shifted)]
        right = [turn(o, d) for o in odds]
        left = [turn(e, -d) for e in evens[:n]] if level < LEVELS - 1 else []
        row = [jnp.where(bit, e, o) for e, o in zip(evens[:n], right)]
        row += [jnp.where(bit, e, o) for e, o in zip(left, odds)]
        if level > 0:
            row.append(jnp.where(bit, evens[n], right[n]))
        return row

    def synthesize(self, low, high, level):
        a = [i - Q * j for i, j in zip(low, high)]
        b = [j + Q * i for i, j in zip(low, high)]
        return self.join(a, b, level)

    def fill(self, edges, item, value):
        at, by, every = EDGE[item]
        l = (self.l - by) & (LANES - 1)
        here = (((l - 64 - HALO) & (LANES - 1)) < 64) & ((l & (every - 1)) == 0)
        edges[at] = jnp.where(here, turn(value, by), edges[at])


class Stacks:
    def __init__(self, block):
        self.block = block
        self.kinds = {}

    def of(self, count):
        if count not in self.kinds:
            self.kinds[count] = Lanes(count * self.block)
        return self.kinds[count]

    def stack(self, rows):
        return [jnp.concatenate(list(v), 0) if len(v) > 1 else v[0] for v in zip(*rows)]

    def unstack(self, row, count):
        return [[v[self.block * i : self.block * (i + 1)] for v in row] for i in range(count)]

    def analyze(self, rows, level):
        n = len(rows)
        low, high = self.of(n).analyze(self.stack(rows), level)
        return self.unstack(low, n), self.unstack(high, n)

    def low(self, rows, level):
        n = len(rows)
        return self.unstack(self.of(n).low(self.stack(rows), level), n)

    def join(self, a, b, level):
        n = len(a)
        return self.unstack(self.of(n).join(self.stack(a), self.stack(b), level), n)

    def synthesize(self, low, high, level):
        n = len(low)
        return self.unstack(self.of(n).synthesize(self.stack(low), self.stack(high), level), n)


def plus(x, y, scale=1.0):
    return [i + (j if scale == 1.0 else scale * j) for i, j in zip(x, y)]


def times(scale, x):
    return [scale * i for i in x]


def mul(x, y):
    return [i * j for i, j in zip(x, y)]


def pair(x0, x1):
    return plus(x1, x0, -T), plus(x0, x1, T)


def unpair(a, b):
    return plus(b, a, -T), plus(a, b, T)


def read_row(x_refs, left_ref, right_ref, lon, lons, k):
    rows = k.l.shape[0]
    row = [x_ref[pl.ds(lon, rows, stride=lons), :] for x_ref in x_refs]
    group, within = divmod(lon, lons // 4)
    beyond = turn(right_ref[within], -HALO * group)
    before = turn(left_ref[within], LANES - HALO - HALO * group)
    row.append(jnp.where(k.l < LANES // 2, beyond, before))
    return row


def put(ref, at, values):
    for i, v in enumerate(values):
        ref[:, pl.ds(LANES * (at + i), LANES)] = v


def get(ref, at, count):
    return [ref[:, pl.ds(LANES * (at + i), LANES)] for i in range(count)]


def first_kernel(lons, block, x_refs, table_ref, to_left_ref, to_right_ref, a_ref, b_ref):
    k = Lanes(block)
    groups = lons // 4

    def row(lon):
        return [x_ref[pl.ds(lon, block, stride=lons), :] for x_ref in x_refs]

    put(b_ref, 0, pair(row(0), row(1))[1])
    put(a_ref, 0, pair(row(lons - 2), row(lons - 1))[0])
    at = pl.ds(pl.multiple_of(pl.program_id(0) * block, block), block)
    for within in range(groups):
        to_left = to_right = None
        for group in range(4):
            lon = groups * group + within
            here = (k.l >> 5) == group
            a = turn(x_refs[0][pl.ds(lon, block, stride=lons), :], HALO * group)
            b = turn(x_refs[-1][pl.ds(lon, block, stride=lons), :], HALO * group - (LANES - HALO))
            to_left = a if to_left is None else jnp.where(here, a, to_left)
            to_right = b if to_right is None else jnp.where(here, b, to_right)
        to_left_ref[within] = to_left
        to_right_ref[within, at, :] = to_right

    @pl.when(pl.program_id(0) == 0)
    def _():
        members = to_right_ref.shape[1] - SUB
        for within in range(groups):
            to_right_ref[within, pl.ds(members, SUB), :] = table_ref[...]


def weights_kernel(index_ref, table_ref, halo_ref, out_ref, arranged_ref):
    l = lax.broadcasted_iota(jnp.int32, (SUB, LANES), 1)
    block = out_ref.shape[1]
    table = get(table_ref, 0, table_ref.shape[1] // LANES)
    halo = jnp.where(l >= LANES - 16, halo_ref[0], 0.0)
    for level in range(LEVELS):
        scale = tap_1 ** (4 * (level + 1))
        mains = MAINS[level]
        stride = 2 << level
        count = 64 * len(table) >> level
        step = LANES // stride
        start, size = 0 * l, count * 2
        for bit in range(min(level + 1, 3)):
            size = size // 2
            start = start + size * ((l >> bit) & 1)
        for j in range(mains):
            k = (start + step * j + l // stride) << level
            value = jnp.zeros((SUB, LANES), jnp.float32)
            for v in range(len(table)):
                value = jnp.where((k >> 7) == v, pick(table[v], k & 127), value)
            arranged_ref[j] = value * scale
        edge = pick(halo, 64 + (l >> 1))
        arranged_ref[mains] = jnp.where(l >= LANES - 2 * stride, edge, 0.0) * scale
        for band in range(3 if level < LEVELS - 1 else 4):
            table_row = index_ref[3 * level + band]
            for i in range(mains + 1):
                out_ref[WEIGHTS[level, band] + i] = jnp.broadcast_to(
                    arranged_ref[i, pl.ds(table_row, 1), :], (block, LANES)
                )


def send_kernel(lons, block, x_refs, left_ref, right_ref, c1_ref, to_right, to_left, far_right, far_left):
    k = Lanes(block)
    many = Stacks(block)
    half = lons // 2
    edges_right, edges_left = [k.zero, k.zero], [k.zero]

    def rows(i):
        return pair(
            read_row(x_refs, left_ref, right_ref, 2 * i, lons, k),
            read_row(x_refs, left_ref, right_ref, 2 * i + 1, lons, k),
        )

    c1 = [None] * half
    h0b = b_next = None
    for start in reversed(range(0, half, SEND_STACK)):
        coarse = []
        pairs0 = [rows(i) for i in range(start, start + SEND_STACK)]
        for i in range(start, start + SEND_STACK):
            a = pairs0[i - start][0]
            if i == half - 1:
                k.fill(edges_right, "a0", a[-1])
                coarse.append(a)
            else:
                after = pairs0[i - start + 1][1] if i < start + SEND_STACK - 1 else b_next
                coarse.append(plus(a, after, Q))
        if start == 0:
            coarse.append(pairs0[0][1])
            k.fill(edges_left, "b0", coarse[-1][-1])
        coarse = many.low(coarse, 0)
        c1[start : start + SEND_STACK] = coarse[:SEND_STACK]
        if start == 0:
            h0b = coarse[-1]
        b_next = pairs0[0][1]
    for i in range(half - 1):
        put(c1_ref, 5 * i, c1[i])

    def message(ref, places, edges, item, row):
        put(ref, places[item], row[:-1])
        k.fill(edges, item, row[-1])

    message(to_right, RIGHT, edges_right, "c1", c1[half - 2])
    pairs1 = [pair(c1[2 * i], c1[2 * i + 1]) for i in range(half // 2)]
    message(to_right, RIGHT, edges_right, "a1", pairs1[-2][0])
    b1 = pairs1[0][1]
    message(to_left, LEFT, edges_left, "b1", b1)

    def lows(pairs, level):
        rows = [plus(pairs[i][0], pairs[i + 1][1], Q) for i in range(len(pairs) - 1)] + [pairs[-1][0]]
        return many.low(rows, level)

    c2 = lows(pairs1, 1)
    pairs2 = [pair(c2[2 * i], c2[2 * i + 1]) for i in range(half // 4)]
    message(to_right, RIGHT, edges_right, "a2", pairs2[-2][0])
    b2 = pairs2[0][1]
    message(to_left, LEFT, edges_left, "b2", b2)
    c3 = lows(pairs2, 2)
    a3, b3 = pair(c3[0], c3[1])
    put(far_right, 0, a3)
    message(to_left, LEFT, edges_left, "b3", b3)

    d1 = times(Q, h0b)
    d2 = many.low([times(Q * T, d1), plus(d1, b1, Q)], 1)
    da, db = pair(d2[0], d2[1])
    d3 = many.low([times(Q, db), plus(da, b2, Q)], 2)
    ka, kb = pair(d3[0], d3[1])
    message(to_right, RIGHT, edges_right, "k", ka)
    put(far_left, 0, kb)
    put(to_right, RIGHT["edge"], edges_right)
    put(to_left, LEFT["edge"], edges_left)


def inner_kernel(lons, block, w_ref, x_refs, left_ref, right_ref, out_ref):
    k = Lanes(block)
    half = lons // 2

    def weight(band):
        return [w_ref[WEIGHTS[0, band] + i] for i in range(5)]

    def store(p, a, b):
        y0, y1 = unpair(a, b)
        put(out_ref, 2 * p * len(a), y0)
        put(out_ref, (2 * p + 1) * len(a), y1)

    def rows(i):
        return pair(
            read_row(x_refs, left_ref, right_ref, 2 * i, lons, k),
            read_row(x_refs, left_ref, right_ref, 2 * i + 1, lons, k),
        )

    many = Stacks(block)
    a, _ = rows(0)
    before = [k.zero] * (len(a) - 1)
    for start in range(0, half - 1, INNER_STACK):
        count = min(INNER_STACK, half - 1 - start)
        lows, highs = [], []
        for p in range(start, start + count):
            a_next, b_next = rows(p + 1)
            lows.append(plus(a, b_next, Q))
            highs.append(plus(b_next, a, -Q))
            a = a_next
        h, g = many.analyze(highs + lows, 0)
        a_sum, b_sum = [], []
        for n in range(count):
            hh, hg, lg = mul(h[n], weight(1)), mul(g[n], weight(2)), mul(g[count + n], weight(0))
            a_sum.append(plus(hh, hg, -Q))
            b_sum.append(plus(hg, hh, Q))
            a_sum.append(times(-Q, lg))
            b_sum.append(lg)
        joined = many.join(a_sum, b_sum, 0)
        for n in range(count):
            z, y = joined[2 * n : 2 * n + 2]
            store(start + n, plus(y, z, -Q), before)
            before = plus(z, y, Q)
    store(half - 1, [k.zero] * len(before), before)


def outer_kernel(
    lons,
    block,
    w_ref,
    part_ref,
    c1_ref,
    own_a,
    own_b,
    own_right,
    own_left,
    left_a,
    right_b,
    from_left,
    from_right,
    far_left,
    far_right,
    out_ref,
    y_ref,
):
    many = Stacks(block)
    half = lons // 2

    def edge(ref, name, places):
        at, by, _ = EDGE[name]
        return turn(get(ref, places["edge"] + at, 1)[0], -by)

    def item(ref, name, places):
        return get(ref, places[name], COUNT[name]) + [edge(ref, name, places)]

    def weight(level, band):
        return [w_ref[WEIGHTS[level, band] + i] for i in range(MAINS[level] + 1)]

    def inner(level, rows, a_first, b_last):
        pairs = [pair(rows[2 * i], rows[2 * i + 1]) for i in range(len(rows) // 2)]
        a = [a_first] + [p[0] for p in pairs]
        b = [p[1] for p in pairs] + [b_last]
        n = len(a)
        h, g = many.analyze(
            [plus(j, i, -Q) for i, j in zip(a, b)] + [plus(i, j, Q) for i, j in zip(a, b)], level
        )
        highs = [
            (mul(h[i], weight(level, 1)), mul(g[i], weight(level, 2))) for i in range(n)
        ]
        return h[n:], [mul(g[n + i], weight(level, 0)) for i in range(n)], highs

    def outer(level, coarse, band_0, highs):
        n = len(coarse)
        rows = many.synthesize(coarse + [h[0] for h in highs], band_0 + [h[1] for h in highs], level)
        a = [plus(rows[i], rows[n + i], -Q) for i in range(n)]
        b = [plus(rows[n + i], rows[i], Q) for i in range(n)]
        field = []
        for i in range(1, n):
            field.extend(unpair(a[i], b[i - 1]))
        return field

    count = own_a.shape[1] // LANES
    a_first = get(left_a, 0, count) + [edge(from_left, "a0", RIGHT)]
    b_first = get(own_b, 0, count) + [edge(own_left, "b0", LEFT)]
    a_last = get(own_a, 0, count) + [edge(own_right, "a0", RIGHT)]
    b_last = get(right_b, 0, count) + [edge(from_right, "b0", LEFT)]
    h, g = many.analyze(
        [plus(a_first, b_first, Q), plus(a_last, b_last, Q), plus(b_first, a_first, -Q), plus(b_last, a_last, -Q)], 0
    )
    g_first, g_last = mul(g[0], weight(0, 0)), mul(g[1], weight(0, 0))
    straddling = [(mul(h[i], weight(0, 1)), mul(g[i], weight(0, 2))) for i in (2, 3)]

    c1 = [item(from_left, "c1", RIGHT), h[0]]
    c1 += [get(c1_ref, 5 * i, 5) for i in range(half - 1)]
    c1.append(h[1])
    c2, g1, z1 = inner(1, c1, item(from_left, "a1", RIGHT), item(from_right, "b1", LEFT))
    c3, g2, z2 = inner(2, c2, item(from_left, "a2", RIGHT), item(from_right, "b2", LEFT))
    a3 = plus(get(far_left, 0, 2), item(from_left, "k", RIGHT))
    b3 = plus(item(from_right, "b3", LEFT), get(far_right, 0, 2))
    c4, g3, z3 = inner(3, c3, a3, b3)
    field = [mul(c, weight(3, 3)) for c in c4]
    for level, g_rows, z_rows in ((3, g3, z3), (2, g2, z2), (1, g1, z1)):
        field = outer(level, field, g_rows, z_rows)
    field = field[1:]

    a_rows, b_rows = list(field), [times(Q, f) for f in field]
    a_rows[0], b_rows[0] = plus(field[0], g_first, -Q), plus(g_first, field[0], Q)
    a_rows[-1], b_rows[-1] = plus(field[-1], g_last, -Q), plus(g_last, field[-1], Q)
    for hh, hg in straddling:
        a_rows.append(plus(hh, hg, -Q))
        b_rows.append(plus(hg, hh, Q))
    joined = []
    for start in range(0, len(a_rows), OUTER_STACK):
        joined += many.join(a_rows[start : start + OUTER_STACK], b_rows[start : start + OUTER_STACK], 0)
    low, (z_first, z_last) = joined[: half + 1], joined[half + 1 :]

    b = plus(z_first, low[0], Q)
    for p in range(half):
        if p < half - 1:
            a = low[p + 1]
            b_next = times(Q, a)
        else:
            a = plus(low[p + 1], z_last, -Q)
        for j, y in enumerate(unpair(a, b)):
            part = get(part_ref, (2 * p + j) * len(y), len(y))
            for v in range(len(y)):
                y_ref[v, pl.ds(block * (2 * p + j), block), :] = part[v] + y[v]
        b = b_next
    for v in range(y_ref.shape[0]):
        for member in range(block):
            out_ref[pl.ds(lons * member, lons), pl.ds(LANES * v, LANES)] = y_ref[
                v, pl.ds(member, lons, stride=block), :
            ]


def shift(x, axis, by, cyclic):
    size = lax.axis_size(axis)
    if cyclic:
        pairs = [(i, (i + by) % size) for i in range(size)]
    else:
        pairs = [(i, i + by) for i in range(size) if 0 <= i + by < size]
    return lax.ppermute(x, axis, pairs)


def per_device(perturbation, weight_table, band_index):
    members, lons, lats = perturbation.shape
    assert lons == 16 and lats == 8 * LANES and members % BLOCK == 0
    block = BLOCK
    steps = members // block
    x = perturbation.reshape(members * lons, lats)
    shape = lambda *dims: jax.ShapeDtypeStruct(dims, jnp.float32)
    groups = lons // 4
    cols = lats // LANES
    params = pltpu.CompilerParams(vmem_limit_bytes=60 * 1024 * 1024)
    by_member = lambda width: pl.BlockSpec((block, width), lambda i: (i, 0))
    x_specs = [pl.BlockSpec((block * lons, LANES), lambda i, v=v: (i, v)) for v in range(cols)]
    halo_spec = pl.BlockSpec((groups, block, LANES), lambda i: (0, i, 0))
    w_spec = pl.BlockSpec((WEIGHT_COUNT, block, LANES), lambda i: (0, 0, 0))

    to_left, to_right, own_a, own_b = pl.pallas_call(
        lambda *refs: first_kernel(lons, block, refs[:cols], *refs[cols:]),
        grid=(steps,),
        in_specs=x_specs + [pl.BlockSpec((SUB, LANES), lambda i: (0, lats // 2 // LANES - 1))],
        out_specs=[
            halo_spec,
            pl.BlockSpec((groups, members + SUB, LANES), lambda i: (0, 0, 0)),
            by_member(lats),
            by_member(lats),
        ],
        out_shape=[
            shape(groups, members, LANES),
            shape(groups, members + SUB, LANES),
            shape(members, lats),
            shape(members, lats),
        ],
        compiler_params=params,
        name="first",
    )(*[x] * cols, weight_table)
    before = shift(to_right, "lat", 1, False)
    beyond = shift(to_left, "lat", -1, False)
    left_a = shift(own_a, "lon", 1, True)
    right_b = shift(own_b, "lon", -1, True)

    weights = pl.pallas_call(
        weights_kernel,
        grid=(1,),
        in_specs=[
            pl.BlockSpec(memory_space=pltpu.SMEM),
            pl.BlockSpec((SUB, lats // 2), lambda i: (0, 0)),
            pl.BlockSpec((1, SUB, LANES), lambda i: (0, members // SUB, 0)),
        ],
        out_specs=pl.BlockSpec((WEIGHT_COUNT, block, LANES), lambda i: (0, 0, 0)),
        out_shape=shape(WEIGHT_COUNT, block, LANES),
        scratch_shapes=[pltpu.VMEM((5, SUB, LANES), jnp.float32)],
        compiler_params=params,
        name="weights",
    )(band_index, weight_table, before)

    c1_width = (lons // 2 - 1) * 5 * LANES
    right_width, left_width = RIGHT_SIZE * LANES, LEFT_SIZE * LANES
    c1, to_right, to_left, far_right, far_left = pl.pallas_call(
        lambda *refs: send_kernel(lons, block, refs[:cols], *refs[cols:]),
        grid=(steps,),
        in_specs=x_specs + [halo_spec, halo_spec],
        out_specs=[by_member(c1_width), by_member(right_width), by_member(left_width)] + [by_member(2 * LANES)] * 2,
        out_shape=[
            shape(members, c1_width),
            shape(members, right_width),
            shape(members, left_width),
            shape(members, 2 * LANES),
            shape(members, 2 * LANES),
        ],
        compiler_params=params,
        cost_estimate=pl.CostEstimate(flops=10**7, bytes_accessed=10**7, transcendentals=0),
        name="send",
    )(*[x] * cols, before, beyond)
    from_left = shift(to_right, "lon", 1, True)
    from_right = shift(to_left, "lon", -1, True)
    from_far_left = shift(far_right, "lon", 2, True)
    from_far_right = shift(far_left, "lon", -2, True)

    part = pl.pallas_call(
        lambda *refs: inner_kernel(lons, block, refs[0], refs[1 : cols + 1], *refs[cols + 1 :]),
        grid=(steps,),
        in_specs=[w_spec] + x_specs + [halo_spec, halo_spec],
        out_specs=by_member(lons * lats),
        out_shape=shape(members, lons * lats),
        compiler_params=params,
        cost_estimate=pl.CostEstimate(flops=10**7, bytes_accessed=4 * 10**7, transcendentals=0),
        name="inner",
    )(weights, *[x] * cols, before, beyond)

    out = pl.pallas_call(
        lambda *refs: outer_kernel(lons, block, *refs),
        grid=(steps,),
        in_specs=[w_spec, by_member(lons * lats), by_member(c1_width), by_member(lats), by_member(lats)]
        + [by_member(right_width), by_member(left_width), by_member(lats), by_member(lats)]
        + [by_member(right_width), by_member(left_width)]
        + [by_member(2 * LANES)] * 2,
        out_specs=pl.BlockSpec((block * lons, lats), lambda i: (i, 0)),
        out_shape=shape(members * lons, lats),
        scratch_shapes=[pltpu.VMEM((cols, block * lons, LANES), jnp.float32)],
        compiler_params=params,
        name="outer",
    )(
        weights,
        part,
        c1,
        own_a,
        own_b,
        to_right,
        to_left,
        left_a,
        right_b,
        from_left,
        from_right,
        from_far_left,
        from_far_right,
    )
    return out.reshape(members, lons, lats)


def solution(mesh):
    placed = (P(None, "lon", "lat"), P(None, "lat"), P())

    return jax.shard_map(per_device, mesh=mesh, in_specs=placed, out_specs=P(None, "lon", "lat"), check_vma=False)
```

```python
import math

import jax
import jax.numpy as jnp
from jax import lax
from jax.experimental import pallas as pl
from jax.experimental.pallas import tpu as pltpu
from jax.sharding import PartitionSpec as P


LEVELS = 4
LANES = 128
SUB = 8
FIRST_BLOCK = 40
SEND_BLOCK = 40
INNER_BLOCK = 40
OUTER_BLOCK = 40
SEND_STACK = 4
INNER_STACK = 2
OUTER_STACK = 6
HALO = 32

root_three = math.sqrt(3.0)
tap_1 = (3.0 + root_three) / (4.0 * math.sqrt(2.0))
tap_2 = (3.0 - root_three) / (4.0 * math.sqrt(2.0))
tap_3 = (1.0 - root_three) / (4.0 * math.sqrt(2.0))
T = tap_3 / tap_2
Q = tap_2 / tap_1


RIGHT = {"c1": 0, "a1": 4, "a2": 8, "k": 10, "edge": 11}
LEFT = {"b1": 0, "b2": 4, "b3": 6, "edge": 7}
RIGHT_SIZE = 13
LEFT_SIZE = 8
EDGE = {
    "c1": (0, 0, 2),
    "a1": (0, 1, 2),
    "a0": (0, 64, 1),
    "a2": (1, 0, 4),
    "k": (1, 1, 8),
    "b1": (0, 0, 2),
    "b2": (0, 1, 4),
    "b3": (0, 3, 8),
    "b0": (0, 64, 1),
}
COUNT = {"c1": 4, "a1": 4, "b1": 4, "a2": 2, "b2": 2, "k": 1, "b3": 1}
MAINS = (4, 2, 1, 1)
WEIGHTS = {}
WEIGHT_COUNT = 0
for level_at in range(LEVELS):
    for band_at in range(3 if level_at < LEVELS - 1 else 4):
        WEIGHTS[level_at, band_at] = WEIGHT_COUNT
        WEIGHT_COUNT += MAINS[level_at] + 1


def turn(v, by):
    by = by % LANES
    return v if by == 0 else pltpu.roll(v, by, 1)


def pick(v, index):
    return jnp.take_along_axis(v, index, axis=1, mode="promise_in_bounds")


class Lanes:
    def __init__(self, rows):
        l = lax.broadcasted_iota(jnp.int32, (rows, LANES), 1)
        self.rows = rows
        self.l = l
        self.zero = jnp.zeros((rows, LANES), jnp.float32)
        self.bit = [(l & (1 << level)) == 0 for level in range(LEVELS)]
        self.ahead, self.behind = [], []
        for level in range(LEVELS):
            stride = 2 << level
            bits = min(level + 1, 3)
            ahead, behind = (l + stride) & (LANES - 1), (l - stride) & (LANES - 1)
            flip = lambda x: int(format(x, "0%db" % bits)[::-1], 2)
            for x in range(1 << bits):
                after = flip((flip(x) + 1) % (1 << bits))
                ahead = jnp.where(l == LANES - stride + x, after, ahead)
                behind = jnp.where(l == after, LANES - stride + x, behind)
            self.ahead.append(ahead)
            self.behind.append(behind)

    def split(self, row, level):
        main, edge = row[:-1], row[-1]
        d, stride, bit, l = 1 << level, 2 << level, self.bit[level], self.l
        half = len(main) // 2
        right = [turn(main[j + half], d) for j in range(half)]
        left = [turn(main[j], -d) for j in range(half)] or [turn(main[0], -d)]
        left.append(turn(edge, -d))
        if half:
            evens = [jnp.where(bit, main[j], right[j]) for j in range(half)]
            odds = [jnp.where(bit, left[j], main[j + half]) for j in range(half)]
        else:
            evens, odds = [main[0]], [left[0]]
        evens.append(edge)
        odds.append(left[-1])
        a = [o - T * e for e, o in zip(evens, odds)]
        b = [e + T * o for e, o in zip(evens, odds)]
        n = len(b) - 1
        first, beyond = b[0], b[-1]
        shifted = [turn(jnp.where(l < stride, b[j + 1], b[j]), -stride) for j in range(n - 1)]
        m = jnp.where(l == 0, beyond, first)
        shifted.append(pick(m if n == 1 else jnp.where(l < stride, m, b[n - 1]), self.ahead[level]))
        shifted.append(turn(jnp.where(l == 0, first, beyond), -stride))
        return a, shifted

    def analyze(self, row, level):
        a, b = self.split(row, level)
        return [i + Q * j for i, j in zip(a, b)], [j - Q * i for i, j in zip(a, b)]

    def low(self, row, level):
        a, b = self.split(row, level)
        return [i + Q * j for i, j in zip(a, b)]

    def join(self, a, b, level):
        d, stride, bit, l = 1 << level, 2 << level, self.bit[level], self.l
        n = len(b) - 1
        top = l >= LANES - stride
        before = turn(b[-1], stride)
        m = b[0] if n == 1 else jnp.where(top, b[n - 1], b[0])
        shifted = [pick(m, self.behind[level])]
        shifted += [turn(jnp.where(top, b[j - 1], b[j]), stride) for j in range(1, n)]
        shifted[0] = jnp.where(l == 0, before, shifted[0])
        if level > 0:
            shifted.append(before)
        evens = [s - T * i for i, s in zip(a, shifted)]
        odds = [i + T * s for i, s in zip(a, shifted)]
        right = [turn(o, d) for o in odds]
        left = [turn(e, -d) for e in evens[:n]] if level < LEVELS - 1 else []
        row = [jnp.where(bit, e, o) for e, o in zip(evens[:n], right)]
        row += [jnp.where(bit, e, o) for e, o in zip(left, odds)]
        if level > 0:
            row.append(jnp.where(bit, evens[n], right[n]))
        return row

    def synthesize(self, low, high, level):
        a = [i - Q * j for i, j in zip(low, high)]
        b = [j + Q * i for i, j in zip(low, high)]
        return self.join(a, b, level)

    def fill(self, edges, item, value):
        at, by, every = EDGE[item]
        l = (self.l - by) & (LANES - 1)
        here = (((l - 64 - HALO) & (LANES - 1)) < 64) & ((l & (every - 1)) == 0)
        edges[at] = jnp.where(here, turn(value, by), edges[at])


class Stacks:
    def __init__(self, block):
        self.block = block
        self.kinds = {}

    def of(self, count):
        if count not in self.kinds:
            self.kinds[count] = Lanes(count * self.block)
        return self.kinds[count]

    def stack(self, rows):
        return [jnp.concatenate(list(v), 0) if len(v) > 1 else v[0] for v in zip(*rows)]

    def unstack(self, row, count):
        return [[v[self.block * i : self.block * (i + 1)] for v in row] for i in range(count)]

    def analyze(self, rows, level):
        n = len(rows)
        low, high = self.of(n).analyze(self.stack(rows), level)
        return self.unstack(low, n), self.unstack(high, n)

    def low(self, rows, level):
        n = len(rows)
        return self.unstack(self.of(n).low(self.stack(rows), level), n)

    def join(self, a, b, level):
        n = len(a)
        return self.unstack(self.of(n).join(self.stack(a), self.stack(b), level), n)

    def synthesize(self, low, high, level):
        n = len(low)
        return self.unstack(self.of(n).synthesize(self.stack(low), self.stack(high), level), n)


def plus(x, y, scale=1.0):
    return [i + (j if scale == 1.0 else scale * j) for i, j in zip(x, y)]


def times(scale, x):
    return [scale * i for i in x]


def mul(x, y):
    return [i * j for i, j in zip(x, y)]


def pair(x0, x1):
    return plus(x1, x0, -T), plus(x0, x1, T)


def unpair(a, b):
    return plus(b, a, -T), plus(a, b, T)


class View:
    def __init__(self, ref, block):
        self.ref = ref
        self.block = block

    def rows(self):
        return pl.ds(pl.multiple_of(pl.program_id(0) * self.block, self.block), self.block)

    def put(self, at, values):
        for i, v in enumerate(values):
            self.ref[at + i, self.rows(), :] = v

    def get(self, at, count):
        return [self.ref[at + i, self.rows(), :] for i in range(count)]


def views(block, refs):
    return [View(ref, block) for ref in refs]


def weight_of(w_ref, block, level, band):
    at = WEIGHTS[level, band]
    return [jnp.concatenate([w_ref[at + i]] * (block // SUB), 0) for i in range(MAINS[level] + 1)]


def put(view, at, values):
    view.put(at, values)


def get(view, at, count):
    return view.get(at, count)


def read_row(x_view, left_view, right_view, lon, lons, k):
    cols = x_view.ref.shape[0] // lons
    row = x_view.get(lon * cols, cols)
    group, within = divmod(lon, lons // 4)
    beyond = turn(right_view.get(within, 1)[0], -HALO * group)
    before = turn(left_view.get(within, 1)[0], LANES - HALO - HALO * group)
    row.append(jnp.where(k.l < LANES // 2, beyond, before))
    return row


def first_kernel(lons, block, x_refs, table_ref, x_out, to_left_ref, to_right_ref, a_ref, b_ref):
    k = Lanes(block)
    x_out, to_left_out, to_right_out, a_out, b_out = views(block, (x_out, to_left_ref, to_right_ref, a_ref, b_ref))
    groups = lons // 4
    cols = len(x_refs)
    edges = []
    kept = {}
    for lon in range(lons):
        row = [x_ref[pl.ds(lon, block, stride=lons), :] for x_ref in x_refs]
        x_out.put(lon * cols, row)
        edges.append((row[0], row[-1]))
        if lon in (0, lons - 2):
            kept[lon] = row
        if lon == 1:
            b_out.put(0, pair(kept[0], row)[1])
        if lon == lons - 1:
            a_out.put(0, pair(kept[lons - 2], row)[0])
    for within in range(groups):
        to_left = to_right = None
        for group in range(4):
            here = (k.l >> 5) == group
            a, b = edges[groups * group + within]
            a, b = turn(a, HALO * group), turn(b, HALO * group - (LANES - HALO))
            to_left = a if to_left is None else jnp.where(here, a, to_left)
            to_right = b if to_right is None else jnp.where(here, b, to_right)
        to_left_out.put(within, [to_left])
        to_right_out.put(within, [to_right])

    @pl.when(pl.program_id(0) == 0)
    def _():
        members = to_right_ref.shape[1] - SUB
        for within in range(groups):
            to_right_ref[within, pl.ds(members, SUB), :] = table_ref[...]


def weights_kernel(index_ref, table_ref, halo_ref, out_ref, arranged_ref):
    l = lax.broadcasted_iota(jnp.int32, (SUB, LANES), 1)
    table = [table_ref[:, pl.ds(LANES * v, LANES)] for v in range(table_ref.shape[1] // LANES)]
    halo = jnp.where(l >= LANES - 16, halo_ref[0, pl.ds(halo_ref.shape[1] - SUB, SUB), :], 0.0)
    for level in range(LEVELS):
        scale = tap_1 ** (4 * (level + 1))
        mains = MAINS[level]
        stride = 2 << level
        count = 64 * len(table) >> level
        step = LANES // stride
        start, size = 0 * l, count * 2
        for bit in range(min(level + 1, 3)):
            size = size // 2
            start = start + size * ((l >> bit) & 1)
        for j in range(mains):
            k = (start + step * j + l // stride) << level
            value = jnp.zeros((SUB, LANES), jnp.float32)
            for v in range(len(table)):
                value = jnp.where((k >> 7) == v, pick(table[v], k & 127), value)
            arranged_ref[j] = value * scale
        edge = pick(halo, 64 + (l >> 1))
        arranged_ref[mains] = jnp.where(l >= LANES - 2 * stride, edge, 0.0) * scale
        for band in range(3 if level < LEVELS - 1 else 4):
            table_row = index_ref[3 * level + band]
            for i in range(mains + 1):
                out_ref[WEIGHTS[level, band] + i] = jnp.broadcast_to(
                    arranged_ref[i, pl.ds(table_row, 1), :], (SUB, LANES)
                )


def send_kernel(lons, block, *refs):
    x_refs, left_ref, right_ref, c1_ref, to_right, to_left, far_right, far_left = views(block, refs)
    k = Lanes(block)
    many = Stacks(block)
    half = lons // 2
    edges_right, edges_left = [k.zero, k.zero], [k.zero]

    def rows(i):
        return pair(
            read_row(x_refs, left_ref, right_ref, 2 * i, lons, k),
            read_row(x_refs, left_ref, right_ref, 2 * i + 1, lons, k),
        )

    c1 = [None] * half
    h0b = b_next = None
    for start in reversed(range(0, half, SEND_STACK)):
        coarse = []
        pairs0 = [rows(i) for i in range(start, start + SEND_STACK)]
        for i in range(start, start + SEND_STACK):
            a = pairs0[i - start][0]
            if i == half - 1:
                k.fill(edges_right, "a0", a[-1])
                coarse.append(a)
            else:
                after = pairs0[i - start + 1][1] if i < start + SEND_STACK - 1 else b_next
                coarse.append(plus(a, after, Q))
        if start == 0:
            coarse.append(pairs0[0][1])
            k.fill(edges_left, "b0", coarse[-1][-1])
        coarse = many.low(coarse, 0)
        c1[start : start + SEND_STACK] = coarse[:SEND_STACK]
        if start == 0:
            h0b = coarse[-1]
        b_next = pairs0[0][1]
    for i in range(half - 1):
        put(c1_ref, 5 * i, c1[i])

    def message(ref, places, edges, item, row):
        put(ref, places[item], row[:-1])
        k.fill(edges, item, row[-1])

    message(to_right, RIGHT, edges_right, "c1", c1[half - 2])
    pairs1 = [pair(c1[2 * i], c1[2 * i + 1]) for i in range(half // 2)]
    message(to_right, RIGHT, edges_right, "a1", pairs1[-2][0])
    b1 = pairs1[0][1]
    message(to_left, LEFT, edges_left, "b1", b1)

    def lows(pairs, level):
        rows = [plus(pairs[i][0], pairs[i + 1][1], Q) for i in range(len(pairs) - 1)] + [pairs[-1][0]]
        return many.low(rows, level)

    c2 = lows(pairs1, 1)
    pairs2 = [pair(c2[2 * i], c2[2 * i + 1]) for i in range(half // 4)]
    message(to_right, RIGHT, edges_right, "a2", pairs2[-2][0])
    b2 = pairs2[0][1]
    message(to_left, LEFT, edges_left, "b2", b2)
    c3 = lows(pairs2, 2)
    a3, b3 = pair(c3[0], c3[1])
    put(far_right, 0, a3)
    message(to_left, LEFT, edges_left, "b3", b3)

    d1 = times(Q, h0b)
    d2 = many.low([times(Q * T, d1), plus(d1, b1, Q)], 1)
    da, db = pair(d2[0], d2[1])
    d3 = many.low([times(Q, db), plus(da, b2, Q)], 2)
    ka, kb = pair(d3[0], d3[1])
    message(to_right, RIGHT, edges_right, "k", ka)
    put(far_left, 0, kb)
    put(to_right, RIGHT["edge"], edges_right)
    put(to_left, LEFT["edge"], edges_left)


def inner_kernel(lons, block, w_ref, *refs):
    x_refs, left_ref, right_ref, out_ref = views(block, refs)
    k = Lanes(block)
    half = lons // 2

    def weight(band):
        return weight_of(w_ref, block, 0, band)

    def store(p, a, b):
        y0, y1 = unpair(a, b)
        put(out_ref, 2 * p * len(a), y0)
        put(out_ref, (2 * p + 1) * len(a), y1)

    def rows(i):
        return pair(
            read_row(x_refs, left_ref, right_ref, 2 * i, lons, k),
            read_row(x_refs, left_ref, right_ref, 2 * i + 1, lons, k),
        )

    many = Stacks(block)
    a, _ = rows(0)
    before = [k.zero] * (len(a) - 1)
    for start in range(0, half - 1, INNER_STACK):
        count = min(INNER_STACK, half - 1 - start)
        lows, highs = [], []
        for p in range(start, start + count):
            a_next, b_next = rows(p + 1)
            lows.append(plus(a, b_next, Q))
            highs.append(plus(b_next, a, -Q))
            a = a_next
        h, g = many.analyze(highs + lows, 0)
        a_sum, b_sum = [], []
        for n in range(count):
            hh, hg, lg = mul(h[n], weight(1)), mul(g[n], weight(2)), mul(g[count + n], weight(0))
            a_sum.append(plus(hh, hg, -Q))
            b_sum.append(plus(hg, hh, Q))
            a_sum.append(times(-Q, lg))
            b_sum.append(lg)
        joined = many.join(a_sum, b_sum, 0)
        for n in range(count):
            z, y = joined[2 * n : 2 * n + 2]
            store(start + n, plus(y, z, -Q), before)
            before = plus(z, y, Q)
    store(half - 1, [k.zero] * len(before), before)


def outer_kernel(lons, block, w_ref, *refs):
    part_ref, c1_ref, own_a, own_b, own_right, own_left = views(block, refs[:6])
    left_a, right_b, from_left, from_right, far_left, far_right = views(block, refs[6:12])
    out_ref, y_ref = refs[12:]
    many = Stacks(block)
    half = lons // 2

    def edge(ref, name, places):
        at, by, _ = EDGE[name]
        return turn(get(ref, places["edge"] + at, 1)[0], -by)

    def item(ref, name, places):
        return get(ref, places[name], COUNT[name]) + [edge(ref, name, places)]

    def weight(level, band):
        return weight_of(w_ref, block, level, band)

    def inner(level, rows, a_first, b_last):
        pairs = [pair(rows[2 * i], rows[2 * i + 1]) for i in range(len(rows) // 2)]
        a = [a_first] + [p[0] for p in pairs]
        b = [p[1] for p in pairs] + [b_last]
        n = len(a)
        h, g = many.analyze(
            [plus(j, i, -Q) for i, j in zip(a, b)] + [plus(i, j, Q) for i, j in zip(a, b)], level
        )
        highs = [
            (mul(h[i], weight(level, 1)), mul(g[i], weight(level, 2))) for i in range(n)
        ]
        return h[n:], [mul(g[n + i], weight(level, 0)) for i in range(n)], highs

    def outer(level, coarse, band_0, highs):
        n = len(coarse)
        rows = many.synthesize(coarse + [h[0] for h in highs], band_0 + [h[1] for h in highs], level)
        a = [plus(rows[i], rows[n + i], -Q) for i in range(n)]
        b = [plus(rows[n + i], rows[i], Q) for i in range(n)]
        field = []
        for i in range(1, n):
            field.extend(unpair(a[i], b[i - 1]))
        return field

    count = own_a.ref.shape[0]
    a_first = get(left_a, 0, count) + [edge(from_left, "a0", RIGHT)]
    b_first = get(own_b, 0, count) + [edge(own_left, "b0", LEFT)]
    a_last = get(own_a, 0, count) + [edge(own_right, "a0", RIGHT)]
    b_last = get(right_b, 0, count) + [edge(from_right, "b0", LEFT)]
    h, g = many.analyze(
        [plus(a_first, b_first, Q), plus(a_last, b_last, Q), plus(b_first, a_first, -Q), plus(b_last, a_last, -Q)], 0
    )
    g_first, g_last = mul(g[0], weight(0, 0)), mul(g[1], weight(0, 0))
    straddling = [(mul(h[i], weight(0, 1)), mul(g[i], weight(0, 2))) for i in (2, 3)]

    c1 = [item(from_left, "c1", RIGHT), h[0]]
    c1 += [get(c1_ref, 5 * i, 5) for i in range(half - 1)]
    c1.append(h[1])
    c2, g1, z1 = inner(1, c1, item(from_left, "a1", RIGHT), item(from_right, "b1", LEFT))
    c3, g2, z2 = inner(2, c2, item(from_left, "a2", RIGHT), item(from_right, "b2", LEFT))
    a3 = plus(get(far_left, 0, 2), item(from_left, "k", RIGHT))
    b3 = plus(item(from_right, "b3", LEFT), get(far_right, 0, 2))
    c4, g3, z3 = inner(3, c3, a3, b3)
    field = [mul(c, weight(3, 3)) for c in c4]
    for level, g_rows, z_rows in ((3, g3, z3), (2, g2, z2), (1, g1, z1)):
        field = outer(level, field, g_rows, z_rows)
    field = field[1:]

    a_rows, b_rows = list(field), [times(Q, f) for f in field]
    a_rows[0], b_rows[0] = plus(field[0], g_first, -Q), plus(g_first, field[0], Q)
    a_rows[-1], b_rows[-1] = plus(field[-1], g_last, -Q), plus(g_last, field[-1], Q)
    for hh, hg in straddling:
        a_rows.append(plus(hh, hg, -Q))
        b_rows.append(plus(hg, hh, Q))
    joined = []
    for start in range(0, len(a_rows), OUTER_STACK):
        joined += many.join(a_rows[start : start + OUTER_STACK], b_rows[start : start + OUTER_STACK], 0)
    low, (z_first, z_last) = joined[: half + 1], joined[half + 1 :]

    b = plus(z_first, low[0], Q)
    for p in range(half):
        if p < half - 1:
            a = low[p + 1]
            b_next = times(Q, a)
        else:
            a = plus(low[p + 1], z_last, -Q)
        for j, y in enumerate(unpair(a, b)):
            part = get(part_ref, (2 * p + j) * len(y), len(y))
            for v in range(len(y)):
                y_ref[v, pl.ds(block * (2 * p + j), block), :] = part[v] + y[v]
        b = b_next
    for v in range(y_ref.shape[0]):
        for member in range(block):
            out_ref[pl.ds(lons * member, lons), pl.ds(LANES * v, LANES)] = y_ref[
                v, pl.ds(member, lons, stride=block), :
            ]


def shift(x, axis, by, cyclic):
    size = lax.axis_size(axis)
    if cyclic:
        pairs = [(i, (i + by) % size) for i in range(size)]
    else:
        pairs = [(i, i + by) for i in range(size) if 0 <= i + by < size]
    return lax.ppermute(x, axis, pairs)


def per_device(perturbation, weight_table, band_index):
    members, lons, lats = perturbation.shape
    assert lons == 16 and lats == 8 * LANES and members % SUB == 0
    x = perturbation.reshape(members * lons, lats)
    registers = lambda count, rows=members: jax.ShapeDtypeStruct((count, rows, LANES), jnp.float32)
    whole = pl.BlockSpec(memory_space=pltpu.VMEM)
    groups = lons // 4
    cols = lats // LANES

    def call(kernel, block, outs, megabytes, **more):
        block = block if members % block == 0 else SUB
        return pl.pallas_call(
            lambda *refs: kernel(lons, block, *refs),
            grid=(members // block,),
            out_shape=outs,
            compiler_params=pltpu.CompilerParams(vmem_limit_bytes=megabytes * 1024 * 1024),
            **more,
        )

    block = FIRST_BLOCK if members % FIRST_BLOCK == 0 else SUB
    xt, to_left, to_right, own_a, own_b = call(
        lambda lons, block, *refs: first_kernel(lons, block, refs[:cols], *refs[cols:]),
        FIRST_BLOCK,
        [registers(lons * cols), registers(groups), registers(groups, members + SUB), registers(cols), registers(cols)],
        24,
        in_specs=[pl.BlockSpec((block * lons, LANES), lambda i, v=v: (i, v)) for v in range(cols)]
        + [pl.BlockSpec((SUB, LANES), lambda i: (0, lats // 2 // LANES - 1))],
        out_specs=[whole] * 5,
    )(*[pltpu.with_memory_space_constraint(x, pltpu.HBM)] * cols, pltpu.with_memory_space_constraint(weight_table, pltpu.HBM))
    before = shift(to_right, "lat", 1, False)
    beyond = shift(to_left, "lat", -1, False)
    left_a = shift(own_a, "lon", 1, True)
    right_b = shift(own_b, "lon", -1, True)

    weights = pl.pallas_call(
        weights_kernel,
        in_specs=[pl.BlockSpec(memory_space=pltpu.SMEM), whole, whole],
        out_specs=whole,
        out_shape=registers(WEIGHT_COUNT, SUB),
        scratch_shapes=[pltpu.VMEM((5, SUB, LANES), jnp.float32)],
        compiler_params=pltpu.CompilerParams(vmem_limit_bytes=8 * 1024 * 1024),
        name="weights",
    )(band_index, weight_table, before)

    c1, to_right, to_left, far_right, far_left = call(
        send_kernel,
        SEND_BLOCK,
        [registers(n) for n in ((lons // 2 - 1) * 5, RIGHT_SIZE, LEFT_SIZE, 2, 2)],
        24,
        in_specs=[whole] * 3,
        out_specs=[whole] * 5,
        cost_estimate=pl.CostEstimate(flops=10**7, bytes_accessed=10**7, transcendentals=0),
    )(xt, before, beyond)
    from_left = shift(to_right, "lon", 1, True)
    from_right = shift(to_left, "lon", -1, True)
    from_far_left = shift(far_right, "lon", 2, True)
    from_far_right = shift(far_left, "lon", -2, True)

    part = call(
        inner_kernel,
        INNER_BLOCK,
        registers(lons * cols),
        24,
        in_specs=[whole] * 4,
        out_specs=whole,
        cost_estimate=pl.CostEstimate(flops=10**7, bytes_accessed=4 * 10**7, transcendentals=0),
    )(weights, xt, before, beyond)

    block = OUTER_BLOCK if members % OUTER_BLOCK == 0 else SUB
    out = call(
        outer_kernel,
        OUTER_BLOCK,
        jax.ShapeDtypeStruct((members * lons, lats), jnp.float32),
        28,
        in_specs=[whole] * 13,
        out_specs=pl.BlockSpec((block * lons, lats), lambda i: (i, 0)),
        scratch_shapes=[pltpu.VMEM((cols, block * lons, LANES), jnp.float32)],
    )(
        weights,
        part,
        c1,
        own_a,
        own_b,
        to_right,
        to_left,
        left_a,
        right_b,
        from_left,
        from_right,
        from_far_left,
        from_far_right,
    )
    return out.reshape(members, lons, lats)


def solution(mesh):
    placed = (P(None, "lon", "lat"), P(None, "lat"), P())

    return jax.shard_map(per_device, mesh=mesh, in_specs=placed, out_specs=P(None, "lon", "lat"), check_vma=False)
```

```python
import math

import jax
import jax.numpy as jnp
from jax import lax
from jax.experimental import pallas as pl
from jax.experimental.pallas import tpu as pltpu
from jax.sharding import PartitionSpec as P


LEVELS = 4
LANES = 128
SUB = 8
FIRST_BLOCK = 40
MIDDLE_BLOCK = 80
INNER_BLOCK = 80
PARTS = 2
SEND_STACK = 4
INNER_STACK = 2
OUTER_STACK = 9
HALO = 32

root_three = math.sqrt(3.0)
tap_1 = (3.0 + root_three) / (4.0 * math.sqrt(2.0))
tap_2 = (3.0 - root_three) / (4.0 * math.sqrt(2.0))
tap_3 = (1.0 - root_three) / (4.0 * math.sqrt(2.0))
T = tap_3 / tap_2
Q = tap_2 / tap_1


RIGHT = {"edge": 0}
LEFT = {"edge": 0}
RIGHT_LATE = {"c1": 0, "a1": 4, "a2": 8, "k": 10}
LEFT_LATE = {"b1": 0, "b2": 4, "b3": 6}
RIGHT_SIZE, RIGHT_LATE_SIZE = 2, 11
LEFT_SIZE, LEFT_LATE_SIZE = 1, 7
READY = 3
EDGE = {
    "c1": (0, 0, 2),
    "a1": (0, 1, 2),
    "a0": (0, 64, 1),
    "a2": (1, 0, 4),
    "k": (1, 1, 8),
    "b1": (0, 0, 2),
    "b2": (0, 1, 4),
    "b3": (0, 3, 8),
    "b0": (0, 64, 1),
}
COUNT = {"c1": 4, "a1": 4, "b1": 4, "a2": 2, "b2": 2, "k": 1, "b3": 1}
MAINS = (4, 2, 1, 1)
WEIGHTS = {}
WEIGHT_COUNT = 0
for level_at in range(LEVELS):
    for band_at in range(3 if level_at < LEVELS - 1 else 4):
        WEIGHTS[level_at, band_at] = WEIGHT_COUNT
        WEIGHT_COUNT += MAINS[level_at] + 1


def turn(v, by):
    by = by % LANES
    return v if by == 0 else pltpu.roll(v, by, 1)


def pick(v, index):
    return jnp.take_along_axis(v, index, axis=1, mode="promise_in_bounds")


class Lanes:
    def __init__(self, rows):
        l = lax.broadcasted_iota(jnp.int32, (rows, LANES), 1)
        self.rows = rows
        self.l = l
        self.zero = jnp.zeros((rows, LANES), jnp.float32)
        self.bit = [(l & (1 << level)) == 0 for level in range(LEVELS)]
        self.ahead, self.behind = [], []
        for level in range(LEVELS):
            stride = 2 << level
            bits = min(level + 1, 3)
            ahead, behind = (l + stride) & (LANES - 1), (l - stride) & (LANES - 1)
            flip = lambda x: int(format(x, "0%db" % bits)[::-1], 2)
            for x in range(1 << bits):
                after = flip((flip(x) + 1) % (1 << bits))
                ahead = jnp.where(l == LANES - stride + x, after, ahead)
                behind = jnp.where(l == after, LANES - stride + x, behind)
            self.ahead.append(ahead)
            self.behind.append(behind)

    def split(self, row, level):
        main, edge = row[:-1], row[-1]
        d, stride, bit, l = 1 << level, 2 << level, self.bit[level], self.l
        half = len(main) // 2
        right = [turn(main[j + half], d) for j in range(half)]
        left = [turn(main[j], -d) for j in range(half)] or [turn(main[0], -d)]
        left.append(turn(edge, -d))
        if half:
            evens = [jnp.where(bit, main[j], right[j]) for j in range(half)]
            odds = [jnp.where(bit, left[j], main[j + half]) for j in range(half)]
        else:
            evens, odds = [main[0]], [left[0]]
        evens.append(edge)
        odds.append(left[-1])
        a = [o - T * e for e, o in zip(evens, odds)]
        b = [e + T * o for e, o in zip(evens, odds)]
        n = len(b) - 1
        first, beyond = b[0], b[-1]
        shifted = [turn(jnp.where(l < stride, b[j + 1], b[j]), -stride) for j in range(n - 1)]
        m = jnp.where(l == 0, beyond, first)
        shifted.append(pick(m if n == 1 else jnp.where(l < stride, m, b[n - 1]), self.ahead[level]))
        shifted.append(turn(jnp.where(l == 0, first, beyond), -stride))
        return a, shifted

    def analyze(self, row, level):
        a, b = self.split(row, level)
        return [i + Q * j for i, j in zip(a, b)], [j - Q * i for i, j in zip(a, b)]

    def low(self, row, level):
        a, b = self.split(row, level)
        return [i + Q * j for i, j in zip(a, b)]

    def join(self, a, b, level):
        d, stride, bit, l = 1 << level, 2 << level, self.bit[level], self.l
        n = len(b) - 1
        top = l >= LANES - stride
        before = turn(b[-1], stride)
        m = b[0] if n == 1 else jnp.where(top, b[n - 1], b[0])
        shifted = [pick(m, self.behind[level])]
        shifted += [turn(jnp.where(top, b[j - 1], b[j]), stride) for j in range(1, n)]
        shifted[0] = jnp.where(l == 0, before, shifted[0])
        if level > 0:
            shifted.append(before)
        evens = [s - T * i for i, s in zip(a, shifted)]
        odds = [i + T * s for i, s in zip(a, shifted)]
        right = [turn(o, d) for o in odds]
        left = [turn(e, -d) for e in evens[:n]] if level < LEVELS - 1 else []
        row = [jnp.where(bit, e, o) for e, o in zip(evens[:n], right)]
        row += [jnp.where(bit, e, o) for e, o in zip(left, odds)]
        if level > 0:
            row.append(jnp.where(bit, evens[n], right[n]))
        return row

    def synthesize(self, low, high, level):
        a = [i - Q * j for i, j in zip(low, high)]
        b = [j + Q * i for i, j in zip(low, high)]
        return self.join(a, b, level)

    def fill(self, edges, item, value):
        at, by, every = EDGE[item]
        l = (self.l - by) & (LANES - 1)
        here = (((l - 64 - HALO) & (LANES - 1)) < 64) & ((l & (every - 1)) == 0)
        edges[at] = jnp.where(here, turn(value, by), edges[at])


class Stacks:
    def __init__(self, block):
        self.block = block
        self.kinds = {}

    def of(self, count):
        if count not in self.kinds:
            self.kinds[count] = Lanes(count * self.block)
        return self.kinds[count]

    def stack(self, rows):
        return [jnp.concatenate(list(v), 0) if len(v) > 1 else v[0] for v in zip(*rows)]

    def unstack(self, row, count):
        return [[v[self.block * i : self.block * (i + 1)] for v in row] for i in range(count)]

    def analyze(self, rows, level):
        n = len(rows)
        low, high = self.of(n).analyze(self.stack(rows), level)
        return self.unstack(low, n), self.unstack(high, n)

    def low(self, rows, level):
        n = len(rows)
        return self.unstack(self.of(n).low(self.stack(rows), level), n)

    def join(self, a, b, level):
        n = len(a)
        return self.unstack(self.of(n).join(self.stack(a), self.stack(b), level), n)

    def synthesize(self, low, high, level):
        n = len(low)
        return self.unstack(self.of(n).synthesize(self.stack(low), self.stack(high), level), n)


def plus(x, y, scale=1.0):
    return [i + (j if scale == 1.0 else scale * j) for i, j in zip(x, y)]


def times(scale, x):
    return [scale * i for i in x]


def mul(x, y):
    return [i * j for i, j in zip(x, y)]


def pair(x0, x1):
    return plus(x1, x0, -T), plus(x0, x1, T)


def unpair(a, b):
    return plus(b, a, -T), plus(a, b, T)


class View:
    def __init__(self, ref, block, start=0):
        self.ref = ref
        self.block = block
        self.start = start

    def rows(self):
        return pl.ds(pl.multiple_of(pl.program_id(0) * self.block + self.start, SUB), self.block)

    def put(self, at, values):
        for i, v in enumerate(values):
            self.ref[at + i, self.rows(), :] = v

    def get(self, at, count):
        return [self.ref[at + i, self.rows(), :] for i in range(count)]


class Parts:
    def __init__(self, refs):
        self.refs = refs

    def put(self, at, values):
        for i, v in enumerate(values):
            row = 0
            for ref in self.refs:
                ref[at + i] = v[row : row + ref.shape[1]]
                row += ref.shape[1]


def views(block, refs, start=0):
    return [View(ref, block, start) for ref in refs]


def weight_of(w_ref, block, level, band):
    at = WEIGHTS[level, band]
    return [jnp.concatenate([w_ref[at + i]] * (block // SUB), 0) for i in range(MAINS[level] + 1)]


def put(view, at, values):
    view.put(at, values)


def read_row(x_view, left_view, right_view, lon, lons, k):
    cols = x_view.ref.shape[0] // lons
    row = x_view.get(lon * cols, cols)
    group, within = divmod(lon, lons // 4)
    beyond = turn(right_view.get(within, 1)[0], -HALO * group)
    before = turn(left_view.get(within, 1)[0], LANES - HALO - HALO * group)
    row.append(jnp.where(k.l < LANES // 2, beyond, before))
    return row


def first_kernel(lons, block, x_refs, table_ref, x_out, to_left_ref, to_right_ref, a_ref, b_ref):
    k = Lanes(block)
    x_out, to_left_out, to_right_out, a_out, b_out = views(block, (x_out, to_left_ref, to_right_ref, a_ref, b_ref))
    groups = lons // 4
    cols = len(x_refs)
    edges = []
    kept = {}
    for lon in range(lons):
        row = [x_ref[pl.ds(lon, block, stride=lons), :] for x_ref in x_refs]
        x_out.put(lon * cols, row)
        edges.append((row[0], row[-1]))
        if lon in (0, lons - 2):
            kept[lon] = row
        if lon == 1:
            b_out.put(0, pair(kept[0], row)[1])
        if lon == lons - 1:
            a_out.put(0, pair(kept[lons - 2], row)[0])
    for within in range(groups):
        to_left = to_right = None
        for group in range(4):
            here = (k.l >> 5) == group
            a, b = edges[groups * group + within]
            a, b = turn(a, HALO * group), turn(b, HALO * group - (LANES - HALO))
            to_left = a if to_left is None else jnp.where(here, a, to_left)
            to_right = b if to_right is None else jnp.where(here, b, to_right)
        to_left_out.put(within, [to_left])
        to_right_out.put(within, [to_right])

    @pl.when(pl.program_id(0) == 0)
    def _():
        members = to_right_ref.shape[1] - SUB
        for within in range(groups):
            to_right_ref[within, pl.ds(members, SUB), :] = table_ref[...]


def weights_kernel(index_ref, table_ref, halo_ref, out_ref, arranged_ref):
    l = lax.broadcasted_iota(jnp.int32, (SUB, LANES), 1)
    table = [table_ref[:, pl.ds(LANES * v, LANES)] for v in range(table_ref.shape[1] // LANES)]
    halo = jnp.where(l >= LANES - 16, halo_ref[0, pl.ds(halo_ref.shape[1] - SUB, SUB), :], 0.0)
    for level in range(LEVELS):
        scale = tap_1 ** (4 * (level + 1))
        mains = MAINS[level]
        stride = 2 << level
        count = 64 * len(table) >> level
        step = LANES // stride
        start, size = 0 * l, count * 2
        for bit in range(min(level + 1, 3)):
            size = size // 2
            start = start + size * ((l >> bit) & 1)
        for j in range(mains):
            k = (start + step * j + l // stride) << level
            value = jnp.zeros((SUB, LANES), jnp.float32)
            for v in range(len(table)):
                value = jnp.where((k >> 7) == v, pick(table[v], k & 127), value)
            arranged_ref[j] = value * scale
        edge = pick(halo, 64 + (l >> 1))
        arranged_ref[mains] = jnp.where(l >= LANES - 2 * stride, edge, 0.0) * scale
        for band in range(3 if level < LEVELS - 1 else 4):
            table_row = index_ref[3 * level + band]
            for i in range(mains + 1):
                out_ref[WEIGHTS[level, band] + i] = jnp.broadcast_to(
                    arranged_ref[i, pl.ds(table_row, 1), :], (SUB, LANES)
                )


def send_kernel(lons, block, *refs):
    x_refs, left_ref, right_ref, c1_ref, to_right, to_left, far_right, far_left, late_left = views(block, refs[:9])
    late_right = Parts(refs[9:])
    k = Lanes(block)
    many = Stacks(block)
    half = lons // 2
    edges_right, edges_left = [k.zero, k.zero], [k.zero]

    def rows(i):
        return pair(
            read_row(x_refs, left_ref, right_ref, 2 * i, lons, k),
            read_row(x_refs, left_ref, right_ref, 2 * i + 1, lons, k),
        )

    c1 = [None] * half
    h0b = b_next = None
    for start in reversed(range(0, half, SEND_STACK)):
        coarse = []
        pairs0 = [rows(i) for i in range(start, start + SEND_STACK)]
        for i in range(start, start + SEND_STACK):
            a = pairs0[i - start][0]
            if i == half - 1:
                k.fill(edges_right, "a0", a[-1])
                coarse.append(a)
            else:
                after = pairs0[i - start + 1][1] if i < start + SEND_STACK - 1 else b_next
                coarse.append(plus(a, after, Q))
        if start == 0:
            coarse.append(pairs0[0][1])
            k.fill(edges_left, "b0", coarse[-1][-1])
        coarse = many.low(coarse, 0)
        c1[start : start + SEND_STACK] = coarse[:SEND_STACK]
        if start == 0:
            h0b = coarse[-1]
        b_next = pairs0[0][1]
    for i in range(half - 1):
        put(c1_ref, 5 * i, c1[i])

    def message(ref, places, edges, item, row):
        put(ref, places[item], row[:-1])
        k.fill(edges, item, row[-1])

    message(late_right, RIGHT_LATE, edges_right, "c1", c1[half - 2])
    pairs1 = [pair(c1[2 * i], c1[2 * i + 1]) for i in range(half // 2)]
    message(late_right, RIGHT_LATE, edges_right, "a1", pairs1[-2][0])
    b1 = pairs1[0][1]
    message(late_left, LEFT_LATE, edges_left, "b1", b1)

    def lows(pairs, level):
        rows = [plus(pairs[i][0], pairs[i + 1][1], Q) for i in range(len(pairs) - 1)] + [pairs[-1][0]]
        return many.low(rows, level)

    c2 = lows(pairs1, 1)
    pairs2 = [pair(c2[2 * i], c2[2 * i + 1]) for i in range(half // 4)]
    message(late_right, RIGHT_LATE, edges_right, "a2", pairs2[-2][0])
    b2 = pairs2[0][1]
    message(late_left, LEFT_LATE, edges_left, "b2", b2)
    c3 = lows(pairs2, 2)
    a3, b3 = pair(c3[0], c3[1])
    put(far_right, 0, a3)
    message(late_left, LEFT_LATE, edges_left, "b3", b3)

    d1 = times(Q, h0b)
    d2 = many.low([times(Q * T, d1), plus(d1, b1, Q)], 1)
    da, db = pair(d2[0], d2[1])
    d3 = many.low([times(Q, db), plus(da, b2, Q)], 2)
    ka, kb = pair(d3[0], d3[1])
    message(late_right, RIGHT_LATE, edges_right, "k", ka)
    put(far_left, 0, kb)
    put(to_right, RIGHT["edge"], edges_right)
    put(to_left, LEFT["edge"], edges_left)


def inner_kernel(lons, block, w_ref, *refs):
    x_refs, left_ref, right_ref, out_ref = views(block, refs)
    k = Lanes(block)
    half = lons // 2

    def weight(band):
        return weight_of(w_ref, block, 0, band)

    def store(p, a, b):
        y0, y1 = unpair(a, b)
        put(out_ref, 2 * p * len(a), y0)
        put(out_ref, (2 * p + 1) * len(a), y1)

    def rows(i):
        return pair(
            read_row(x_refs, left_ref, right_ref, 2 * i, lons, k),
            read_row(x_refs, left_ref, right_ref, 2 * i + 1, lons, k),
        )

    many = Stacks(block)
    a, _ = rows(0)
    before = [k.zero] * (len(a) - 1)
    for start in range(0, half - 1, INNER_STACK):
        count = min(INNER_STACK, half - 1 - start)
        lows, highs = [], []
        for p in range(start, start + count):
            a_next, b_next = rows(p + 1)
            lows.append(plus(a, b_next, Q))
            highs.append(plus(b_next, a, -Q))
            a = a_next
        h, g = many.analyze(highs + lows, 0)
        a_sum, b_sum = [], []
        for n in range(count):
            hh, hg, lg = mul(h[n], weight(1)), mul(g[n], weight(2)), mul(g[count + n], weight(0))
            a_sum.append(plus(hh, hg, -Q))
            b_sum.append(plus(hg, hh, Q))
            a_sum.append(times(-Q, lg))
            b_sum.append(lg)
        joined = many.join(a_sum, b_sum, 0)
        for n in range(count):
            z, y = joined[2 * n : 2 * n + 2]
            store(start + n, plus(y, z, -Q), before)
            before = plus(z, y, Q)
    store(half - 1, [k.zero] * len(before), before)


def edge_of(view, name):
    at, by, _ = EDGE[name]
    return turn(view.get(at, 1)[0], -by)


def steps_of(many, w_ref, block):
    def weight(level, band):
        return weight_of(w_ref, block, level, band)

    def inner(level, a, b):
        n = len(a)
        h, g = many.analyze([plus(j, i, -Q) for i, j in zip(a, b)] + [plus(i, j, Q) for i, j in zip(a, b)], level)
        highs = [(mul(h[i], weight(level, 1)), mul(g[i], weight(level, 2))) for i in range(n)]
        return h[n:], [mul(g[n + i], weight(level, 0)) for i in range(n)], highs

    return weight, inner


MIDDLE = {"c": 0, "g": 10, "z": 20, "c2": 36, "g1": 36 + 3 * READY, "z1": 36 + 6 * READY}
MIDDLE_SIZE = 36 + 11 * READY


def middle_kernel(lons, block, w_ref, *refs):
    c1_ref, own_a, own_b, own_right, own_left, left_a, right_b, from_left, from_right, out = views(block, refs)
    many = Stacks(block)
    half = lons // 2
    _, inner = steps_of(many, w_ref, block)
    count = own_a.ref.shape[0]
    a_first = left_a.get(0, count) + [edge_of(from_left, "a0")]
    b_first = own_b.get(0, count) + [edge_of(own_left, "b0")]
    a_last = own_a.get(0, count) + [edge_of(own_right, "a0")]
    b_last = right_b.get(0, count) + [edge_of(from_right, "b0")]
    coarse, band_0, highs = inner(0, [a_first, a_last], [b_first, b_last])
    z = many.synthesize([h[0] for h in highs], [h[1] for h in highs], 0)
    for i in range(2):
        out.put(MIDDLE["c"] + 5 * i, coarse[i])
        out.put(MIDDLE["g"] + 5 * i, band_0[i])
        out.put(MIDDLE["z"] + 8 * i, z[i])
    c1 = [c1_ref.get(5 * i, 5) for i in range(half - 1)] + [coarse[1]]
    pairs = [pair(c1[2 * i], c1[2 * i + 1]) for i in range(READY + 1)]
    coarse, band_0, highs = inner(1, [p[0] for p in pairs[:-1]], [p[1] for p in pairs[1:]])
    z = many.synthesize([h[0] for h in highs], [h[1] for h in highs], 1)
    for i in range(READY):
        out.put(MIDDLE["c2"] + 3 * i, coarse[i])
        out.put(MIDDLE["g1"] + 3 * i, band_0[i])
        out.put(MIDDLE["z1"] + 5 * i, z[i])


def outer_kernel(lons, block, start, w_ref, *refs):
    part_ref, middle, c1_ref, from_left, from_right, far_left, far_right = views(block, refs[:7], start)
    (late_right,) = views(block, refs[7:8], start)
    (late_left,) = views(block, refs[8:9])
    out_ref, y_ref, stage_ref, sems = refs[-4:]
    many = Stacks(block)
    half = lons // 2
    weight, inner = steps_of(many, w_ref, block)

    def item(view, name, places, edges):
        return view.get(places[name], COUNT[name]) + [edge_of(edges, name)]

    def pairs_of(rows):
        return [pair(rows[2 * i], rows[2 * i + 1]) for i in range(len(rows) // 2)]

    def outer(low_rows, high_rows):
        n = len(low_rows)
        a = [plus(low_rows[i], high_rows[i], -Q) for i in range(n)]
        b = [plus(high_rows[i], low_rows[i], Q) for i in range(n)]
        field = []
        for i in range(1, n):
            field.extend(unpair(a[i], b[i - 1]))
        return field

    c_first, c_last = middle.get(MIDDLE["c"], 5), middle.get(MIDDLE["c"] + 5, 5)
    before = pair(item(late_left, "c1", RIGHT_LATE, from_left), c_first)
    b_own = pair(c1_ref.get(0, 5), c1_ref.get(5, 5))[1]
    a_end = pair(c1_ref.get(5 * (half - 2), 5), c_last)[0]
    c2, g1, z1 = inner(
        1,
        [item(late_left, "a1", RIGHT_LATE, from_left), before[0], a_end],
        [before[1], b_own, item(late_right, "b1", LEFT_LATE, from_right)],
    )
    ready = lambda name, size: [middle.get(MIDDLE[name] + size * i, size) for i in range(READY)]
    c2 = c2[:2] + ready("c2", 3) + c2[2:]
    g1 = g1[:2] + ready("g1", 3) + g1[2:]

    pairs = pairs_of(c2)
    c3, g2, z2 = inner(
        2,
        [item(late_left, "a2", RIGHT_LATE, from_left)] + [p[0] for p in pairs],
        [p[1] for p in pairs] + [item(late_right, "b2", LEFT_LATE, from_right)],
    )
    pairs = pairs_of(c3)
    a3 = plus(far_left.get(0, 2), item(late_left, "k", RIGHT_LATE, from_left))
    b3 = plus(item(late_right, "b3", LEFT_LATE, from_right), far_right.get(0, 2))
    c4, g3, z3 = inner(3, [a3] + [p[0] for p in pairs], [p[1] for p in pairs] + [b3])

    field = [mul(c, weight(3, 3)) for c in c4]
    for level, band_0, highs in ((3, g3, z3), (2, g2, z2), (1, g1, z1)):
        rows = many.synthesize(field + [h[0] for h in highs], band_0 + [h[1] for h in highs], level)
        n = len(field)
        low_rows, high_rows = rows[:n], rows[n:]
        if level == 1:
            high_rows = high_rows[:2] + ready("z1", 5) + high_rows[2:]
        field = outer(low_rows, high_rows)
    field = field[1:]

    g_first, g_last = middle.get(MIDDLE["g"], 5), middle.get(MIDDLE["g"] + 5, 5)
    z_first, z_last = middle.get(MIDDLE["z"], 8), middle.get(MIDDLE["z"] + 8, 8)
    a_rows, b_rows = list(field), [times(Q, f) for f in field]
    a_rows[0], b_rows[0] = plus(field[0], g_first, -Q), plus(g_first, field[0], Q)
    a_rows[-1], b_rows[-1] = plus(field[-1], g_last, -Q), plus(g_last, field[-1], Q)
    low = []
    for n in range(0, len(a_rows), OUTER_STACK):
        low += many.join(a_rows[n : n + OUTER_STACK], b_rows[n : n + OUTER_STACK], 0)

    cols = len(low[0])
    copies = []
    for v in range(cols):
        b = z_first[v] + Q * low[0][v]
        for p in range(half):
            a = low[p + 1][v] if p < half - 1 else low[p + 1][v] - Q * z_last[v]
            for j, y in enumerate((b - T * a, a + T * b)):
                part = part_ref.get((2 * p + j) * cols + v, 1)[0]
                y_ref[v, pl.ds(block * (2 * p + j), block), :] = part + y
            b = Q * a
        for member in range(block):
            stage_ref[v, pl.ds(lons * member, lons), :] = y_ref[v, pl.ds(member, lons, stride=block), :]
        copies.append(
            pltpu.make_async_copy(
                stage_ref.at[v],
                out_ref.at[pl.ds(start * lons, block * lons), pl.ds(LANES * v, LANES)],
                sems.at[v],
            )
        )
        copies[-1].start()
    for copy in copies:
        copy.wait()


def shift(x, axis, by, cyclic):
    size = lax.axis_size(axis)
    if cyclic:
        pairs = [(i, (i + by) % size) for i in range(size)]
    else:
        pairs = [(i, i + by) for i in range(size) if 0 <= i + by < size]
    return lax.ppermute(x, axis, pairs)


def per_device(perturbation, weight_table, band_index):
    members, lons, lats = perturbation.shape
    assert lons == 16 and lats == 8 * LANES and members % SUB == 0
    x = perturbation.reshape(members * lons, lats)
    registers = lambda count, rows=members: jax.ShapeDtypeStruct((count, rows, LANES), jnp.float32)
    whole = pl.BlockSpec(memory_space=pltpu.VMEM)
    groups = lons // 4
    cols = lats // LANES
    tiles = members // SUB
    sizes = [SUB * (tiles * (n + 1) // PARTS - tiles * n // PARTS) for n in range(PARTS)]

    def call(kernel, block, outs, megabytes, **more):
        block = block if members % block == 0 else SUB
        return pl.pallas_call(
            lambda *refs: kernel(lons, block, *refs),
            grid=(members // block,),
            out_shape=outs,
            compiler_params=pltpu.CompilerParams(vmem_limit_bytes=megabytes * 1024 * 1024),
            **more,
        )

    block = FIRST_BLOCK if members % FIRST_BLOCK == 0 else SUB
    xt, to_left, to_right, own_a, own_b = call(
        lambda lons, block, *refs: first_kernel(lons, block, refs[:cols], *refs[cols:]),
        FIRST_BLOCK,
        [registers(lons * cols), registers(groups), registers(groups, members + SUB), registers(cols), registers(cols)],
        24,
        in_specs=[pl.BlockSpec((block * lons, LANES), lambda i, v=v: (i, v)) for v in range(cols)]
        + [pl.BlockSpec((SUB, LANES), lambda i: (0, lats // 2 // LANES - 1))],
        out_specs=[whole] * 5,
    )(*[pltpu.with_memory_space_constraint(x, pltpu.HBM)] * cols, pltpu.with_memory_space_constraint(weight_table, pltpu.HBM))
    before = shift(to_right, "lat", 1, False)
    beyond = shift(to_left, "lat", -1, False)
    left_a = shift(own_a, "lon", 1, True)
    right_b = shift(own_b, "lon", -1, True)

    weights = pl.pallas_call(
        weights_kernel,
        in_specs=[pl.BlockSpec(memory_space=pltpu.SMEM), whole, whole],
        out_specs=whole,
        out_shape=registers(WEIGHT_COUNT, SUB),
        scratch_shapes=[pltpu.VMEM((5, SUB, LANES), jnp.float32)],
        compiler_params=pltpu.CompilerParams(vmem_limit_bytes=8 * 1024 * 1024),
        name="weights",
    )(band_index, weight_table, before)

    c1, to_right, to_left, far_right, far_left, late_left, *late = call(
        send_kernel,
        members,
        [registers(n) for n in ((lons // 2 - 1) * 5, RIGHT_SIZE, LEFT_SIZE, 2, 2, LEFT_LATE_SIZE)]
        + [registers(RIGHT_LATE_SIZE, size) for size in sizes],
        24,
        in_specs=[whole] * 3,
        out_specs=[whole] * (6 + PARTS),
        cost_estimate=pl.CostEstimate(flops=10**7, bytes_accessed=10**7, transcendentals=0),
    )(xt, before, beyond)
    from_left = shift(to_right, "lon", 1, True)
    from_right = shift(to_left, "lon", -1, True)
    late_from_left = []
    for n in range(PARTS):
        late_from_left.append(shift(late[n], "lon", 1, True))
    late_from_right = shift(late_left, "lon", -1, True)
    from_far_left = shift(far_right, "lon", 2, True)
    from_far_right = shift(far_left, "lon", -2, True)

    part = call(
        inner_kernel,
        INNER_BLOCK,
        registers(lons * cols),
        24,
        in_specs=[whole] * 4,
        out_specs=whole,
        cost_estimate=pl.CostEstimate(flops=10**7, bytes_accessed=4 * 10**7, transcendentals=0),
    )(weights, xt, before, beyond)

    middle = call(
        middle_kernel,
        MIDDLE_BLOCK,
        registers(MIDDLE_SIZE),
        20,
        in_specs=[whole] * 10,
        out_specs=whole,
        cost_estimate=pl.CostEstimate(flops=10**7, bytes_accessed=2 * 10**7, transcendentals=0),
    )(weights, c1, own_a, own_b, to_right, to_left, left_a, right_b, from_left, from_right)

    out, start = [], 0
    for n, size in enumerate(sizes):
        out = [
            pl.pallas_call(
                lambda *refs: outer_kernel(lons, size, start, *refs),
                grid=(1,),
                out_shape=jax.ShapeDtypeStruct((members * lons, lats), jnp.float32),
                compiler_params=pltpu.CompilerParams(vmem_limit_bytes=28 * 1024 * 1024),
                in_specs=[whole] * 10 + [pl.BlockSpec(memory_space=pltpu.HBM)] * len(out),
                out_specs=pl.BlockSpec(memory_space=pltpu.HBM),
                scratch_shapes=[
                    pltpu.VMEM((cols, size * lons, LANES), jnp.float32),
                    pltpu.VMEM((cols, size * lons, LANES), jnp.float32),
                    pltpu.SemaphoreType.DMA((cols,)),
                ],
                input_output_aliases={10: 0} if out else {},
                cost_estimate=pl.CostEstimate(flops=10**7, bytes_accessed=10**7, transcendentals=0),
            )(
                weights,
                part,
                middle,
                c1,
                from_left,
                from_right,
                from_far_left,
                from_far_right,
                late_from_right,
                late_from_left[n],
                *out,
            )
        ]
        start += size
    (out,) = out
    return out.reshape(members, lons, lats)


def solution(mesh):
    placed = (P(None, "lon", "lat"), P(None, "lat"), P())

    return jax.shard_map(per_device, mesh=mesh, in_specs=placed, out_specs=P(None, "lon", "lat"), check_vma=False)
```
